32 devices in a mesh: facet: 4 (over z), strip: 8 (over y, x, core).
Axes of the slice: x: 2, y: 2, z: 4, core: 2. Of those that a mesh axis runs over, the one named last changes fastest.
Arguments:
- sky_components: bfloat16 [4, 2, 4, 2048, 2048], P('facet', None, None, 'strip'), may hold values from -6 to 6
- scale_kernels: float32 [4, 33], replicated, may hold values from 0.026111647 to 0.26111647
- row_taper: bfloat16 [4, 2048, 512], P('facet'), may hold values from -0.125 to 0.125
- col_taper: bfloat16 [4, 2048, 1024], P('facet'), may hold values from -0.125 to 0.125
- finish_rows: bfloat16 [4, 512, 128], replicated, may hold values from -0.25 to 0.25
- finish_cols: bfloat16 [4, 512, 128], replicated, may hold values from -0.5 to 0.5
- subgrid_owner: int32 [32], replicated, may hold values from 0 to 31, as said below
- block_cell: int32 [2048, 2], P(('facet', 'strip')), may hold values from 0 to 480
- vis_offset: float32 [2048, 2, 128], P(('facet', 'strip')), may hold values from 0 to 31
- block_owner: int32 [2048, 1], P(('facet', 'strip')), may hold values from 0 to 31; in each aligned block of 64 rows (0 to 63, 64 to 127, ...) at most 4 rows name the same one
- observed: float32 [4096, 2, 128], P(('facet', 'strip')), may hold values from -6 to 6
- antenna_pair_index: int32 [4096, 2, 128], P(('facet', 'strip')), may hold values from 0 to 511
- gains: float32 [2, 512], replicated, may hold values from 0.1 to 1.9
Outputs:
- subgrids: bfloat16 [32, 2, 512, 512], P(('facet', 'strip'))
- residual: float32 [4096, 2, 128], P(('facet', 'strip'))
The draws below stay inside these ranges and needn't reach their ends.
Inputs may be any that keep to these rules, and one draw needn't show every extreme that they name: Every device number appears once; subgrid_owner[a * 8 + b] = rowperm(a) * 8 + colperm(b) for a permutation rowperm of the subgrid rows and a permutation colperm of the subgrid columns. `block_owner`: among the 64 blocks of one device at most 4 share an owner, and some owner takes exactly 4 of them.
All inputs are finite; a program needn't handle non-finite values.
Results may differ from the reference program's by a relative error of at most 0.02.
Values may be sent and summed in bfloat16 or wider, within the bound.
A program may use at most 128 MiB of HBM per device.

```python
import math
import jax
import jax.numpy as jnp
import numpy as np
from jax import lax

FS = 2048
CM = 128
SG = 512
TILE = 32
BLOCK_VISIBILITY = 128
CORRELATION_NUM = 2
SCALES = 4
HALF = 16
ANTENNA_COUNT = 512
BLK = 64
FACETS = 4
SUBROWS = 4
SUBCOLS = 8
SUBGRID_COUNT = 32
RECEIVE_BLOCKS = 4


def draw_subgrid_owner(key, part):
    row_perm = jax.random.permutation(jax.random.fold_in(key, 11), SUBROWS).astype(jnp.int32)
    col_perm = jax.random.permutation(jax.random.fold_in(key, 23), SUBCOLS).astype(jnp.int32)
    grid_ids = jnp.arange(SUBGRID_COUNT, dtype=jnp.int32)
    return (row_perm[grid_ids // SUBCOLS] * SUBCOLS + col_perm[grid_ids % SUBCOLS]).astype(jnp.int32)


def plant(array, own_key, low, largest):
    index_at = [jax.random.randint(jax.random.fold_in(own_key, axis), (), 0, length) for axis, length in enumerate(array.shape)]
    main_axis = array.shape.index(max(array.shape))
    neighbour = index_at[:main_axis] + [(index_at[main_axis] + 1) % array.shape[main_axis]] + index_at[main_axis + 1:]
    return array.at[tuple(index_at)].set(low).at[tuple(neighbour)].set(largest)


def block_scale(key, dims, split, smallest, top_value):
    level, own = 1.0, jax.random.fold_in(key, 6)
    for axis_at, shards_of in split:
        draws = jnp.exp(jax.random.uniform(jax.random.fold_in(own, axis_at), (shards_of,), jnp.float32, smallest / len(split), top_value / len(split)))
        level = level * jnp.repeat(draws, dims[axis_at] // shards_of).reshape([-1 if axis == axis_at else 1 for axis in range(len(dims))])
    return level


def shared_out(rng, own, number, rows, count, top, bound, skew):
    sequence = jax.random.permutation(rng, count)
    crowded, ordinary = shares(count, rows * top, bound, skew, True), shares(count, rows * top, bound, skew, False)
    places = jnp.arange(count)

    def named(tallies, offset_by):
        used = int((tallies > 0).sum())
        fixed = max(1, used // 4)
        passed = fixed + (places - fixed + offset_by * (used - fixed)) % max(1, count - fixed)
        return jnp.zeros((count,), jnp.int32).at[sequence[jnp.where(places < fixed, places, passed)]].set(jnp.asarray(tallies, jnp.int32))

    tallies = jnp.where(number % 4 == 0, named(crowded, number // 4), named(ordinary, number - number // 4 - 1))
    mixed = jax.random.permutation(jax.random.fold_in(own, 3), count)
    giver, taker = mixed[0:count // 2 * 2:2], mixed[1:count // 2 * 2:2]
    slack = jnp.minimum(tallies[giver] - 1, bound - tallies[taker]) // 2
    slack = jnp.where((giver == sequence[0]) | (taker == sequence[0]) | (tallies[taker] == 0), 0, jnp.maximum(slack, 0))
    passed = jax.random.randint(jax.random.fold_in(own, 4), (count // 2,), 0, 1 << 20) % (slack + 1)
    tallies = tallies.at[giver].add(-passed).at[taker].add(passed)
    labels = jnp.searchsorted(jnp.cumsum(tallies), jnp.arange(rows * top), side="right").astype(jnp.int32)
    listing = labels.reshape(top, rows).T
    listing = listing[jax.random.permutation(jax.random.fold_in(own, 1), rows)]
    offset_by = jax.random.randint(jax.random.fold_in(own, 2), (rows, 1), 0, top)
    return jnp.take_along_axis(listing, (jnp.arange(top)[None, :] + offset_by) % top, axis=1)


def shares(number_of, total, limit, lean, full):
    weights = [(1 << 20) // math.isqrt(grade ** lean) + 1 for grade in range(1, number_of + 1)]
    largest = limit if full else min(limit, max(-(-total // number_of), total * weights[0] // sum(weights)))
    least = 1 if total - largest >= number_of - 1 else 0
    holding, surplus = [largest] + [least] * (number_of - 1), total - largest - least * (number_of - 1)
    while surplus > 0:
        candidates = [i for i in range(1, number_of) if holding[i] < largest] or [i for i in range(1, number_of) if holding[i] < limit]
        pool, left = sum([weights[i] for i in candidates]), surplus
        for i in candidates:
            extra = min(limit - holding[i], max(1, left * weights[i] // pool), surplus)
            holding[i] = holding[i] + extra
            surplus = surplus - extra
    return np.array(holding)


def gaussian(rng, shape, deviation, most, pieces=(), kind=jnp.bfloat16):
    values = jax.random.normal(rng, shape, jnp.float32) * deviation
    if len(pieces) > 0:
        values = block_scale(rng, shape, pieces, -0.22, 0.18) * values
    return jnp.clip(values, min=-most, max=most).astype(kind)


def setup_inputs(seed: int = 0) -> dict:
    arg_keys = jax.random.split(jax.random.key(seed), 14)
    sky_components = gaussian(arg_keys[0], (FACETS, CORRELATION_NUM, SCALES, FS, FS), 1.0, 6.0, ((0, 4), (3, 8)))
    scale_kernels = jnp.clip(jnp.exp(jax.random.uniform(arg_keys[1], (SCALES, 2 * HALF + 1), jnp.float32, math.log(0.026111647), math.log(0.26111647))), 0.026111647, 0.26111647)
    row_taper = gaussian(arg_keys[2], (FACETS, FS, SUBROWS * CM), FS ** -0.5, 0.125, ((0, 4),))
    col_taper = gaussian(arg_keys[3], (FACETS, FS, SUBCOLS * CM), FS ** -0.5, 0.125, ((0, 4),))
    finish_rows = gaussian(arg_keys[4], (FACETS, SG, CM), (FACETS * CM) ** -0.5, 0.25)
    finish_cols = gaussian(arg_keys[5], (FACETS, SG, CM), CM ** -0.5, 0.5)
    subgrid_owner = draw_subgrid_owner(jax.random.fold_in(arg_keys[13], 71), 0)
    block_cell = plant(jax.random.randint(arg_keys[7], (SUBGRID_COUNT * BLK, 2), 0, SG - TILE + 1), jax.random.fold_in(arg_keys[7], 1), 0, SG - TILE).astype(jnp.int32)
    vis_offset = jnp.clip(31.0 * jax.random.uniform(arg_keys[8], (SUBGRID_COUNT * BLK, 2, BLOCK_VISIBILITY), jnp.float32) ** block_scale(arg_keys[8], (SUBGRID_COUNT * BLK, 2, BLOCK_VISIBILITY), ((0, 32),), -0.2, 0.2), 0.0, 31.0)
    block_owner_keys = jax.random.split(jax.random.fold_in(arg_keys[9], 1), (SUBGRID_COUNT * BLK) // BLK)
    block_owner_turns = jax.random.permutation(jax.random.fold_in(arg_keys[9], 3), (SUBGRID_COUNT * BLK) // BLK)
    block_owner = jax.vmap(lambda own, number: shared_out(jax.random.fold_in(arg_keys[9], 2), own, number, BLK, SUBGRID_COUNT, 1, RECEIVE_BLOCKS, 2))(block_owner_keys, block_owner_turns).reshape((SUBGRID_COUNT * BLK, 1))
    observed = gaussian(arg_keys[10], (SUBGRID_COUNT * SUBGRID_COUNT * RECEIVE_BLOCKS, CORRELATION_NUM, BLOCK_VISIBILITY), 1.0, 6.0, ((0, 32),), jnp.float32)
    antenna_pair_index = plant(jax.random.randint(arg_keys[11], (SUBGRID_COUNT * SUBGRID_COUNT * RECEIVE_BLOCKS, 2, BLOCK_VISIBILITY), 0, ANTENNA_COUNT), jax.random.fold_in(arg_keys[11], 1), 0, ANTENNA_COUNT - 1).astype(jnp.int32)
    gains = jnp.clip(1.0 + 0.18 * jax.random.normal(arg_keys[12], (CORRELATION_NUM, ANTENNA_COUNT), jnp.float32), 0.1, 1.9)
    return dict(sky_components=sky_components, scale_kernels=scale_kernels, row_taper=row_taper, col_taper=col_taper, finish_rows=finish_rows, finish_cols=finish_cols, subgrid_owner=subgrid_owner, block_cell=block_cell, vis_offset=vis_offset, block_owner=block_owner, observed=observed, antenna_pair_index=antenna_pair_index, gains=gains)


KERNEL_WIDTH = 1.5


def smooth_rows_cols(padded, kernels, rows):
    taps = kernels.shape[1]
    width = (taps - 1) // 2
    along_rows = jnp.zeros(padded.shape[:2] + (rows, padded.shape[3]), jnp.float32)
    for tap in range(taps):
        along_rows = along_rows + kernels[:, tap][None, :, None, None] * padded[:, :, tap:tap + rows, :].astype(jnp.float32)
    cols = along_rows.shape[3]
    wide = jnp.pad(along_rows, ((0, 0), (0, 0), (0, 0), (width, width)))
    total = jnp.zeros_like(along_rows)
    for tap in range(taps):
        total = total + kernels[:, tap][None, :, None, None] * wide[:, :, :, tap:tap + cols]
    return jnp.sum(total, axis=1).astype(jnp.bfloat16)


def weights_of(offset):
    places = jnp.arange(TILE).astype(jnp.float32)
    delta = (places[None, None, :] - offset[:, :, None]) / KERNEL_WIDTH
    return jnp.exp(-0.5 * delta * delta)


def reference(sky_components, scale_kernels, row_taper, col_taper, finish_rows, finish_cols, subgrid_owner, block_cell, vis_offset, block_owner, observed, antenna_pair_index, gains):
    width = HALF

    def one_facet(index):
        comp = sky_components[index]
        padded = jnp.pad(comp, ((0, 0), (0, 0), (width, width), (0, 0)))
        smoothed = smooth_rows_cols(padded, scale_kernels, FS)
        col_products = jnp.einsum('crw,wk->crk', smoothed.astype(jnp.float32), col_taper[index].astype(jnp.float32)).astype(jnp.bfloat16)
        col_products = col_products.reshape(CORRELATION_NUM, FS, SUBCOLS, CM)
        rows_t = row_taper[index].reshape(FS, SUBROWS, CM)
        return jnp.einsum('rai,crbj->cabij', rows_t.astype(jnp.float32), col_products.astype(jnp.float32)).astype(jnp.bfloat16)

    contributions = lax.map(one_facet, jnp.arange(FACETS, dtype=jnp.int32))
    numbers = jnp.arange(SUBGRID_COUNT, dtype=jnp.int32)
    home = jnp.sum(jnp.where(subgrid_owner[None, :] == numbers[:, None], numbers[None, :], 0), axis=1).astype(jnp.int32)

    def one_device(device):
        grid_id = home[device]
        row_id = grid_id // SUBCOLS
        col_id = grid_id % SUBCOLS
        mine = contributions[:, :, row_id, col_id]
        spread = jnp.einsum('fcij,fsj->fcis', mine.astype(jnp.float32), finish_cols.astype(jnp.float32)).astype(jnp.bfloat16)
        subgrid = jnp.einsum('fri,fcis->crs', finish_rows.astype(jnp.float32), spread.astype(jnp.float32)).astype(jnp.bfloat16)
        cells = lax.dynamic_slice_in_dim(block_cell, device * BLK, BLK, 0)
        offsets = lax.dynamic_slice_in_dim(vis_offset, device * BLK, BLK, 0)

        def cut_tile(corner):
            return lax.dynamic_slice(subgrid, (jnp.int32(0), corner[0], corner[1]), (CORRELATION_NUM, TILE, TILE))

        tiles = jax.vmap(cut_tile)(cells)
        row_weights = weights_of(offsets[:, 0, :]).astype(jnp.bfloat16)
        col_weights = weights_of(offsets[:, 1, :])
        partial_value = jnp.einsum('kvi,kcij->kcvj', row_weights.astype(jnp.float32), tiles.astype(jnp.float32))
        predicted = jnp.sum(partial_value * col_weights[:, None, :, :], axis=3)
        return subgrid, predicted

    subgrids, predicted = lax.map(one_device, numbers)
    dest = block_owner[:, 0].reshape(SUBGRID_COUNT, BLK)
    same = dest[:, :, None] == dest[:, None, :]
    order = jnp.arange(BLK, dtype=jnp.int32)
    earlier = order[None, :] < order[:, None]
    rank = jnp.sum((same & earlier[None, :, :]).astype(jnp.int32), axis=2)
    slot = dest * (SUBGRID_COUNT * RECEIVE_BLOCKS) + numbers[:, None] * RECEIVE_BLOCKS + rank
    placed = jnp.zeros(observed.shape, jnp.float32).at[slot.reshape(-1)].set(predicted.reshape(SUBGRID_COUNT * BLK, CORRELATION_NUM, BLOCK_VISIBILITY))
    gain_p = jnp.take(gains, antenna_pair_index[:, 0, :], axis=1)
    gain_q = jnp.take(gains, antenna_pair_index[:, 1, :], axis=1)
    product = jnp.transpose(gain_p * gain_q, (1, 0, 2))
    residual = observed - product * placed
    return subgrids, residual
```

```python
import functools

import jax
import jax.numpy as jnp
from jax import lax
from jax.experimental import pallas as pl
from jax.experimental.pallas import tpu as pltpu
from jax.sharding import PartitionSpec as P

TILE = 32
KERNEL_WIDTH = 1.5
LANES = 128
COL_TILE = 256
ALIGN = 16
TALL = TILE + ALIGN
WIDE = LANES + TILE
MESH = pl.DeviceIdType.MESH
ACROSS = (((1,), (1,)), ((), ()))


def mm(a, b):
    return jnp.dot(a, b, preferred_element_type=jnp.float32)


def fill_bands(taps_ref, pad_ref, across_ref, down_ref, width):
    scales, taps = taps_ref.shape
    span = LANES + taps - 1
    pad_ref[...] = jnp.zeros_like(pad_ref)
    pad_ref[:, 0:taps] = taps_ref[...]
    down_ref[...] = jnp.zeros_like(down_ref)
    for s in range(scales):
        row = jnp.broadcast_to(pad_ref[s : s + 1, :], (LANES, 2 * LANES))
        band = pltpu.roll(row, 0, 1, stride=1, stride_axis=0)
        across_ref[s] = band[:, :span].astype(across_ref.dtype)
        down = band.T[:span].astype(down_ref.dtype)
        for tile in range(COL_TILE // LANES):
            start = LANES - width + tile * LANES
            down_ref[s, start : start + span, tile * LANES : (tile + 1) * LANES] = down


def position_of(values, wanted):
    place = 0
    for j, value in enumerate(values):
        gap = value - wanted
        place += j * jnp.maximum(1 - gap * gap, 0)
    return jnp.minimum(place, len(values) - 1)


def looked_up(row, index):
    low, high = index % LANES, index // LANES
    out = None
    for chunk in range(row.shape[1] // LANES):
        table = jnp.broadcast_to(row[:, chunk * LANES : (chunk + 1) * LANES], index.shape)
        got = jnp.take_along_axis(table, low, axis=1, mode="promise_in_bounds")
        out = got if out is None else jnp.where(high == chunk, got, out)
    return out


def whole_kernel(
    n_facet,
    n_strip,
    owner_ref,
    corner_ref,
    taps_ref,
    dest_ref,
    gains_ref,
    x_ref,
    col_in,
    row_in,
    frows_in,
    fcols_in,
    offset_in,
    index_in,
    observed_in,
    subgrid_out,
    residual_out,
    x_buf,
    col_taper,
    row_taper,
    frows,
    fcols,
    offsets,
    index,
    observed,
    pad_ref,
    across_ref,
    down_ref,
    y_ref,
    smooth_ref,
    stage,
    grouped,
    stage2,
    mine,
    row_mats,
    spread,
    turned,
    subgrid,
    row_weights,
    col_weights,
    onehot,
    values,
    outgoing,
    arrived,
    wide,
    product,
    load_sem,
    halo_send,
    halo_recv,
    strip_send,
    strip_recv,
    facet_send,
    facet_recv,
    vis_send,
    vis_recv,
    out_sem,
    ready_sem,
):
    corr, scales, rows, side = x_ref.shape
    width = (taps_ref.shape[1] - 1) // 2
    tiles = side // COL_TILE
    contrib = fcols.shape[2]
    sub_side = fcols.shape[1]
    blocks = offsets.shape[0]
    vis = offsets.shape[2]
    devices = n_facet * n_strip
    capacity = observed.shape[0] // devices
    sub_cols = col_taper.shape[0]
    sub_rows = row_taper.shape[0]
    f_me = lax.axis_index("facet")
    s_me = lax.axis_index("strip")
    me = f_me * n_strip + s_me

    x_loads = [
        pltpu.make_async_copy(x_ref.at[c], x_buf.at[c, :, pl.ds(width, rows)], load_sem.at[c])
        for c in range(corr)
    ]
    others = [
        pltpu.make_async_copy(src, dst, load_sem.at[corr + n])
        for n, (src, dst) in enumerate(
            (
                (index_in, index),
                (offset_in, offsets),
                (frows_in, frows),
                (fcols_in, fcols),
                (observed_in, observed),
            )
        )
    ]
    index_load, offset_load, frows_load, fcols_load, observed_load = others
    col_loads = [
        pltpu.make_async_copy(
            col_in.at[:, pl.ds(b * contrib, contrib)], col_taper.at[b], load_sem.at[corr + 5 + b]
        )
        for b in range(sub_cols)
    ]
    row_loads = [
        pltpu.make_async_copy(
            row_in.at[:, pl.ds(a * contrib, contrib)],
            row_taper.at[a],
            load_sem.at[corr + 5 + sub_cols + a],
        )
        for a in range(sub_rows)
    ]
    for load in x_loads + col_loads + others + row_loads:
        load.start()

    barrier = pltpu.get_barrier_semaphore()
    for off in range(1, n_strip):
        pl.semaphore_signal(
            barrier, inc=1, device_id={"strip": lax.rem(s_me + off, n_strip)}, device_id_type=MESH
        )
    for off in range(1, n_facet):
        pl.semaphore_signal(
            barrier, inc=1, device_id={"facet": lax.rem(f_me + off, n_facet)}, device_id_type=MESH
        )
    fill_bands(taps_ref, pad_ref, across_ref, down_ref, width)
    y_ref[:, :, 0:LANES] = jnp.zeros((scales, rows, LANES), y_ref.dtype)
    y_ref[:, :, LANES + side : 2 * LANES + side] = jnp.zeros((scales, rows, LANES), y_ref.dtype)
    pl.semaphore_wait(barrier, n_strip + n_facet - 2)
    right, left = lax.rem(s_me + 1, n_strip), lax.rem(s_me + n_strip - 1, n_strip)
    halos = []
    for c in range(corr):
        pair = []
        for way, (start, landing, peer) in enumerate(
            ((rows - width, 0, right), (0, rows + width, left))
        ):
            copy = pltpu.make_async_remote_copy(
                src_ref=x_ref.at[c, :, pl.ds(start, width)],
                dst_ref=x_buf.at[c, :, pl.ds(landing, width)],
                send_sem=halo_send.at[c, way],
                recv_sem=halo_recv.at[c, way],
                device_id={"strip": peer},
                device_id_type=MESH,
            )
            copy.start()
            pair.append(copy)
        halos.append(pair)
    for off in range(1, n_strip):
        pl.semaphore_signal(
            ready_sem, inc=1, device_id={"strip": lax.rem(s_me + off, n_strip)}, device_id_type=MESH
        )
    col_perm = [lax.rem(owner_ref[b], n_strip) for b in range(sub_cols)]
    row_perm = [lax.div(owner_ref[a * sub_cols], n_strip) for a in range(sub_rows)]

    strip_copies = []
    for c in range(corr):
        x_loads[c].wait()
        for copy in halos[c]:
            copy.wait()

        @pl.when(s_me == 0)
        def _():
            x_buf[c, :, 0:width] = jnp.zeros((scales, width, side), x_buf.dtype)

        @pl.when(s_me == n_strip - 1)
        def _():
            x_buf[c, :, rows + width : rows + 2 * width] = jnp.zeros((scales, width, side), x_buf.dtype)

        for s in range(scales):
            for b in range(rows // LANES):
                part = x_buf[c, s, b * LANES : (b + 1) * LANES + 2 * width]
                y_ref[s, b * LANES : (b + 1) * LANES, LANES : LANES + side] = mm(
                    across_ref[s], part
                ).astype(y_ref.dtype)

        def one_tile(tile, carry):
            first = pl.multiple_of(tile * COL_TILE, COL_TILE)
            smoothed = jnp.zeros((rows, COL_TILE), jnp.float32)
            for s in range(scales):
                smoothed += mm(y_ref[s, :, pl.ds(first, COL_TILE + 2 * LANES)], down_ref[s])
            smooth_ref[:, pl.ds(first, COL_TILE)] = smoothed.astype(smooth_ref.dtype)
            return carry

        lax.fori_loop(0, tiles, one_tile, 0, unroll=2)
        if c == 0:
            for load in col_loads:
                load.wait()
        for off in range(1, n_strip + 1):
            peer = lax.rem(s_me + off, n_strip)
            b = position_of(col_perm, peer)
            got = mm(smooth_ref[...], col_taper[b]).astype(stage.dtype)
            if off == n_strip:
                grouped[s_me, c] = got
                continue
            stage[c, off] = got
            copy = pltpu.make_async_remote_copy(
                src_ref=stage.at[c, off],
                dst_ref=grouped.at[s_me, c],
                send_sem=strip_send.at[c, off],
                recv_sem=strip_recv.at[c, off],
                device_id={"strip": peer},
                device_id_type=MESH,
            )
            copy.start()
            strip_copies.append(copy)

    index_load.wait()
    for c in range(corr):
        row = gains_ref[c : c + 1, :]
        product[c] = looked_up(row, index[:, 0, :]) * looked_up(row, index[:, 1, :])
    dest = dest_ref[...]
    k_row = lax.broadcasted_iota(jnp.int32, (blocks, blocks), 0)
    k_col = lax.broadcasted_iota(jnp.int32, (blocks, blocks), 1)
    dest_wide = jnp.broadcast_to(dest, (blocks, blocks))
    dest_tall = jnp.sum(jnp.where(k_row == k_col, dest_wide, 0), axis=1, keepdims=True)
    same = (dest_tall == dest_wide) & (k_row < k_col)
    rank = jnp.sum(jnp.where(same, 1, 0), axis=0, keepdims=True)
    target = dest * capacity + rank
    code = jnp.concatenate([target * corr + c for c in range(corr)], axis=1)
    places = lax.broadcasted_iota(jnp.int32, onehot.shape, 0)
    onehot[...] = jnp.where(places == code, 1.0, 0.0).astype(onehot.dtype)
    r_blocks, q_blocks = sub_side // LANES, sub_side // ALIGN
    turned[:, r_blocks] = jnp.zeros((corr,) + turned.shape[2:], turned.dtype)
    turned[:, :, q_blocks] = jnp.zeros((corr, r_blocks + 1, ALIGN, LANES), turned.dtype)
    offset_load.wait()
    row_places = lax.broadcasted_iota(jnp.int32, (WIDE, vis), 0)
    col_places = lax.broadcasted_iota(jnp.int32, (TALL, vis), 0)
    factor = -0.5 / (KERNEL_WIDTH * KERNEL_WIDTH)

    def weights(spots, offset):
        delta = spots.astype(jnp.float32) - offset
        inside = (spots >= 0) & (spots < TILE)
        return jnp.where(inside, jnp.exp(factor * (delta * delta)), 0.0)

    def corner(k):
        r, q = corner_ref[0, k], corner_ref[1, k]
        rb = jnp.clip(lax.div(r, LANES), 0, r_blocks - 1)
        qb = jnp.clip(lax.div(q, ALIGN), 0, q_blocks - 2)
        return r - rb * LANES, q - qb * ALIGN, rb, qb

    def one_weight(k, carry):
        r_in, q_in, _, _ = corner(k)
        here = offsets[k]
        row_weights[k] = weights(row_places - r_in, here[0:1]).astype(row_weights.dtype)
        col_weights[k] = weights(col_places - q_in, here[1:2])
        return carry

    lax.fori_loop(0, blocks, one_weight, 0, unroll=2)
    frows_load.wait()
    fcols_load.wait()
    row_mats[...] = jnp.concatenate([frows[f] for f in range(n_facet)], axis=1)
    for load in row_loads:
        load.wait()

    facet_copies = []
    for c in range(corr):
        for copy in strip_copies[c * (n_strip - 1) : (c + 1) * (n_strip - 1)]:
            copy.wait()
        flipped = jnp.concatenate([grouped[x, c].T for x in range(n_strip)], axis=1)
        for off in range(1, n_facet + 1):
            peer = lax.rem(f_me + off, n_facet)
            a = position_of(row_perm, peer)
            got = mm(flipped, row_taper[a]).astype(stage2.dtype)
            if off == n_facet:
                mine[f_me, c] = got
                continue
            stage2[c, off] = got
            copy = pltpu.make_async_remote_copy(
                src_ref=stage2.at[c, off],
                dst_ref=mine.at[f_me, c],
                send_sem=facet_send.at[c, off],
                recv_sem=facet_recv.at[c, off],
                device_id={"facet": peer},
                device_id_type=MESH,
            )
            copy.start()
            facet_copies.append(copy)

    for c in range(corr):
        for copy in facet_copies[c * (n_facet - 1) : (c + 1) * (n_facet - 1)]:
            copy.wait()
        for f in range(n_facet):
            spread[c, :, f * contrib : (f + 1) * contrib] = mm(fcols[f], mine[f, c]).astype(spread.dtype)
        for rb in range(r_blocks):
            turned[c, rb, 0:q_blocks] = (
                lax.dot_general(
                    spread[c],
                    row_mats[rb * LANES : (rb + 1) * LANES],
                    ACROSS,
                    preferred_element_type=jnp.float32,
                )
                .astype(turned.dtype)
                .reshape(q_blocks, ALIGN, LANES)
            )

        def one_block(k, carry, c=c):
            _, _, rb, qb = corner(k)
            tile = jnp.concatenate(
                [
                    jnp.concatenate([turned[c, rb + j, qb + i] for j in range(2)], axis=1)
                    for i in range(TALL // ALIGN)
                ],
                axis=0,
            )
            along = mm(tile[:, :WIDE], row_weights[k])
            values[pl.ds(c * blocks + k, 1), :] = jnp.sum(along * col_weights[k], axis=0, keepdims=True)
            return carry

        lax.fori_loop(0, blocks, one_block, 0, unroll=8)

    outgoing[...] = (
        mm(onehot[...], values[...].astype(jnp.bfloat16))
        .astype(outgoing.dtype)
        .reshape(outgoing.shape)
    )
    pl.semaphore_wait(ready_sem, n_strip - 1)

    def vis_copy(off):
        peer = lax.rem(me + off, devices)
        return pltpu.make_async_remote_copy(
            src_ref=outgoing.at[peer],
            dst_ref=arrived.at[me],
            send_sem=vis_send.at[off],
            recv_sem=vis_recv.at[off],
            device_id={"facet": peer // n_strip, "strip": peer % n_strip},
            device_id_type=MESH,
        )

    def send_one(off, carry):
        vis_copy(off).start()
        return carry

    lax.fori_loop(1, devices, send_one, 0)
    arrived[me] = outgoing[me]
    subgrid_copies = []
    for c in range(corr):
        subgrid[c] = lax.dot_general(
            row_mats[...], spread[c], ACROSS, preferred_element_type=jnp.float32
        ).astype(subgrid.dtype)
        copy = pltpu.make_async_copy(subgrid.at[c], subgrid_out.at[c], out_sem.at[c])
        copy.start()
        subgrid_copies.append(copy)
    observed_load.wait()

    def wait_one(off, carry):
        vis_copy(off).wait()
        return carry

    lax.fori_loop(1, devices, wait_one, 0)
    wide[...] = arrived[...].astype(jnp.float32).reshape(wide.shape)
    for c in range(corr):
        placed = wide[pl.ds(c, devices * capacity, stride=corr), :]
        residual_out[:, c, :] = observed[:, c, :] - product[c] * placed
    for copy in subgrid_copies:
        copy.wait()


def on_device(
    sky_components,
    scale_kernels,
    row_taper,
    col_taper,
    finish_rows,
    finish_cols,
    subgrid_owner,
    block_cell,
    vis_offset,
    block_owner,
    observed,
    antenna_pair_index,
    gains,
):
    n_facet = lax.axis_size("facet")
    n_strip = lax.axis_size("strip")
    devices = n_facet * n_strip
    comp = sky_components[0]
    corr, scales, rows, side = comp.shape
    taps = scale_kernels.shape[1]
    sub_side, contrib = finish_cols.shape[1], finish_cols.shape[2]
    blocks, _, vis = vis_offset.shape
    sub_rows, sub_cols = row_taper.shape[2] // contrib, col_taper.shape[2] // contrib
    slots = observed.shape[0]
    per_device = slots // devices * corr
    whole = pl.BlockSpec(memory_space=pltpu.VMEM)
    scalars = pl.BlockSpec(memory_space=pltpu.SMEM)
    remote = pl.BlockSpec(memory_space=pl.ANY)
    bf16, f32 = jnp.bfloat16, jnp.float32
    dma = pltpu.SemaphoreType.DMA
    subgrid, residual = pl.pallas_call(
        functools.partial(whole_kernel, n_facet, n_strip),
        in_specs=[scalars, scalars, whole, whole, whole] + [remote] * 8,
        out_specs=[remote, whole],
        out_shape=[
            jax.ShapeDtypeStruct((corr, sub_side, sub_side), bf16),
            jax.ShapeDtypeStruct(observed.shape, f32),
        ],
        scratch_shapes=[
            pltpu.VMEM((corr, scales, rows + taps - 1, side), bf16),
            pltpu.VMEM((sub_cols, side, contrib), bf16),
            pltpu.VMEM((sub_rows, side, contrib), bf16),
            pltpu.VMEM(finish_rows.shape, bf16),
            pltpu.VMEM(finish_cols.shape, bf16),
            pltpu.VMEM(vis_offset.shape, f32),
            pltpu.VMEM(antenna_pair_index.shape, jnp.int32),
            pltpu.VMEM(observed.shape, f32),
            pltpu.VMEM((scales, 2 * LANES), f32),
            pltpu.VMEM((scales, LANES, LANES + taps - 1), bf16),
            pltpu.VMEM((scales, COL_TILE + 2 * LANES, COL_TILE), bf16),
            pltpu.VMEM((scales, rows, side + 2 * LANES), bf16),
            pltpu.VMEM((rows, side), bf16),
            pltpu.VMEM((corr, n_strip, rows, contrib), bf16),
            pltpu.VMEM((n_strip, corr, rows, contrib), bf16),
            pltpu.VMEM((corr, n_facet, contrib, contrib), bf16),
            pltpu.VMEM((n_facet, corr, contrib, contrib), bf16),
            pltpu.VMEM((sub_side, n_facet * contrib), bf16),
            pltpu.VMEM((corr, sub_side, n_facet * contrib), bf16),
            pltpu.VMEM((corr, sub_side // LANES + 1, sub_side // ALIGN + 1, ALIGN, LANES), bf16),
            pltpu.VMEM((corr, sub_side, sub_side), bf16),
            pltpu.VMEM((blocks, WIDE, vis), bf16),
            pltpu.VMEM((blocks, TALL, vis), f32),
            pltpu.VMEM((devices * per_device, corr * blocks), bf16),
            pltpu.VMEM((corr * blocks, vis), f32),
            pltpu.VMEM((devices, per_device, vis), bf16),
            pltpu.VMEM((devices, per_device, vis), bf16),
            pltpu.VMEM((devices * per_device, vis), f32),
            pltpu.VMEM((corr, slots, vis), f32),
            dma((corr + 5 + sub_cols + sub_rows,)),
            dma((corr, 2)),
            dma((corr, 2)),
            dma((corr, n_strip)),
            dma((corr, n_strip)),
            dma((corr, n_facet)),
            dma((corr, n_facet)),
            dma((devices,)),
            dma((devices,)),
            dma((corr,)),
            pltpu.SemaphoreType.REGULAR,
        ],
        compiler_params=pltpu.CompilerParams(
            collective_id=0, has_side_effects=True, vmem_limit_bytes=60 * 1024 * 1024
        ),
        name="sky_to_residual",
    )(
        subgrid_owner,
        block_cell.T,
        scale_kernels,
        block_owner.reshape(1, blocks),
        gains,
        comp,
        col_taper[0],
        row_taper[0],
        finish_rows,
        finish_cols,
        vis_offset,
        antenna_pair_index,
        observed,
    )
    return subgrid[None], residual


def solution(mesh):
    placed = (
        P("facet", None, None, "strip", None),
        P(),
        P("facet", None, None),
        P("facet", None, None),
        P(),
        P(),
        P(),
        P(("facet", "strip"), None),
        P(("facet", "strip"), None, None),
        P(("facet", "strip"), None),
        P(("facet", "strip"), None, None),
        P(("facet", "strip"), None, None),
        P(),
    )
    return jax.shard_map(
        on_device,
        mesh=mesh,
        in_specs=placed,
        out_specs=(P(("facet", "strip"), None, None, None), P(("facet", "strip"), None, None)),
        check_vma=False,
    )
```

```python
import functools

import jax
import jax.numpy as jnp
from jax import lax
from jax.experimental import pallas as pl
from jax.experimental.pallas import tpu as pltpu
from jax.sharding import PartitionSpec as P

TILE = 32
KERNEL_WIDTH = 1.5
LANES = 128
COL_TILE = 256
ALIGN = 16
TALL = TILE + ALIGN
WIDE = LANES + TILE
MESH = pl.DeviceIdType.MESH
ACROSS = (((1,), (1,)), ((), ()))


def mm(a, b):
    return jnp.dot(a, b, preferred_element_type=jnp.float32)


def fill_bands(taps_ref, pad_ref, across_ref, down_ref, width):
    scales, taps = taps_ref.shape
    tall, rows = across_ref.shape[1:]
    span = LANES + taps - 1
    pad_ref[...] = jnp.zeros_like(pad_ref)
    pad_ref[:, 0:taps] = taps_ref[...]
    down_ref[...] = jnp.zeros_like(down_ref)
    for s in range(scales):
        row = jnp.broadcast_to(pad_ref[s : s + 1, :], (LANES, 2 * LANES))
        band = pltpu.roll(row, 0, 1, stride=1, stride_axis=0)
        down = band.T[:span].astype(down_ref.dtype)
        for tile in range(COL_TILE // LANES):
            start = LANES - width + tile * LANES
            down_ref[s, start : start + span, tile * LANES : (tile + 1) * LANES] = down
        for first in range(0, tall, LANES):
            size = min(LANES, tall - first)
            line = jnp.broadcast_to(pad_ref[s : s + 1, 0:rows], (size, rows))
            line = pltpu.roll(line, (rows + first - 2 * width) % rows, 1)
            line = pltpu.roll(line, 0, 1, stride=1, stride_axis=0)
            gap = (
                lax.broadcasted_iota(jnp.int32, (size, rows), 1)
                - lax.broadcasted_iota(jnp.int32, (size, rows), 0)
                - first
            )
            line = jnp.where((gap <= 0) & (gap >= -2 * width), line, 0.0)
            across_ref[s, first : first + size] = line.astype(across_ref.dtype)


def plus(a, b):
    return (a.astype(jnp.float32) + b.astype(jnp.float32)).astype(a.dtype)


def position_of(values, wanted):
    place = 0
    for j, value in enumerate(values):
        gap = value - wanted
        place += j * jnp.maximum(1 - gap * gap, 0)
    return jnp.minimum(place, len(values) - 1)


def looked_up(row, index):
    low, high = index % LANES, index // LANES
    out = None
    for chunk in range(row.shape[1] // LANES):
        table = jnp.broadcast_to(row[:, chunk * LANES : (chunk + 1) * LANES], index.shape)
        got = jnp.take_along_axis(table, low, axis=1, mode="promise_in_bounds")
        out = got if out is None else jnp.where(high == chunk, got, out)
    return out


def whole_kernel(
    n_facet,
    n_strip,
    owner_ref,
    corner_ref,
    taps_ref,
    dest_ref,
    gains_ref,
    x_ref,
    col_in,
    row_in,
    frows_in,
    fcols_in,
    offset_in,
    index_in,
    observed_in,
    subgrid_out,
    residual_out,
    x_buf,
    col_taper,
    row_taper,
    frows,
    fcols,
    offsets,
    index,
    observed,
    pad_ref,
    across_ref,
    down_ref,
    y_ref,
    smooth_ref,
    stage,
    grouped,
    stage2,
    mine,
    row_mats,
    spread,
    turned,
    subgrid,
    row_weights,
    col_weights,
    onehot,
    values,
    outgoing,
    arrived,
    wide,
    product,
    load_sem,
    strip_send,
    strip_recv,
    facet_send,
    facet_recv,
    vis_send,
    vis_recv,
    out_sem,
    ready_sem,
):
    corr, scales, rows, side = x_ref.shape
    width = (taps_ref.shape[1] - 1) // 2
    tall = rows + 2 * width
    tiles = side // COL_TILE
    contrib = fcols.shape[2]
    sub_side = fcols.shape[1]
    blocks = offsets.shape[0]
    vis = offsets.shape[2]
    devices = n_facet * n_strip
    capacity = observed.shape[0] // devices
    sub_cols = col_taper.shape[0]
    sub_rows = row_taper.shape[0]
    r_blocks, q_blocks = sub_side // LANES, sub_side // ALIGN
    f_me = lax.axis_index("facet")
    s_me = lax.axis_index("strip")
    me = f_me * n_strip + s_me

    x_loads = [
        pltpu.make_async_copy(x_ref.at[c], x_buf.at[c], load_sem.at[c])
        for c in range(corr)
    ]
    others = [
        pltpu.make_async_copy(src, dst, load_sem.at[corr + n])
        for n, (src, dst) in enumerate(
            (
                (index_in, index),
                (offset_in, offsets),
                (frows_in, frows),
                (fcols_in, fcols),
                (observed_in, observed),
            )
        )
    ]
    index_load, offset_load, frows_load, fcols_load, observed_load = others
    col_loads = [
        pltpu.make_async_copy(
            col_in.at[:, pl.ds(b * contrib, contrib)], col_taper.at[b], load_sem.at[corr + 5 + b]
        )
        for b in range(sub_cols)
    ]
    row_loads = [
        pltpu.make_async_copy(
            row_in.at[:, pl.ds(a * contrib, contrib)],
            row_taper.at[a],
            load_sem.at[corr + 5 + sub_cols + a],
        )
        for a in range(sub_rows)
    ]
    for load in x_loads + col_loads + others + row_loads:
        load.start()

    barrier = pltpu.get_barrier_semaphore()
    for off in range(1, n_strip):
        pl.semaphore_signal(
            barrier, inc=1, device_id={"strip": lax.rem(s_me + off, n_strip)}, device_id_type=MESH
        )
    for off in range(1, n_facet):
        pl.semaphore_signal(
            barrier, inc=1, device_id={"facet": lax.rem(f_me + off, n_facet)}, device_id_type=MESH
        )
    fill_bands(taps_ref, pad_ref, across_ref, down_ref, width)
    y_ref[:, :, 0:LANES] = jnp.zeros((scales, tall, LANES), y_ref.dtype)
    y_ref[:, :, LANES + side : 2 * LANES + side] = jnp.zeros((scales, tall, LANES), y_ref.dtype)
    col_perm = [lax.rem(owner_ref[b], n_strip) for b in range(sub_cols)]
    row_perm = [lax.div(owner_ref[a * sub_cols], n_strip) for a in range(sub_rows)]

    strip_copies = []
    for c in range(corr):
        x_loads[c].wait()
        for s in range(scales):
            for n in range(0, side, COL_TILE):
                y_ref[s, :, LANES + n : LANES + n + COL_TILE] = mm(
                    across_ref[s], x_buf[c, s, :, n : n + COL_TILE]
                ).astype(y_ref.dtype)

        def one_tile(tile, carry):
            first = pl.multiple_of(tile * COL_TILE, COL_TILE)
            smoothed = jnp.zeros((tall, COL_TILE), jnp.float32)
            for s in range(scales):
                smoothed += mm(y_ref[s, :, pl.ds(first, COL_TILE + 2 * LANES)], down_ref[s])
            smooth_ref[:, pl.ds(first, COL_TILE)] = smoothed.astype(smooth_ref.dtype)
            return carry

        lax.fori_loop(0, tiles, one_tile, 0, unroll=2)
        if c == 0:
            for load in col_loads:
                load.wait()
            pl.semaphore_wait(barrier, n_strip + n_facet - 2)
            for off in range(1, n_strip):
                pl.semaphore_signal(
                    ready_sem,
                    inc=1,
                    device_id={"strip": lax.rem(s_me + off, n_strip)},
                    device_id_type=MESH,
                )
        for first in range(1, n_strip + 1, 2):
            peers = [lax.rem(s_me + off, n_strip) for off in (first, first + 1)]
            pair = jnp.concatenate([col_taper[position_of(col_perm, peer)] for peer in peers], axis=1)
            got = mm(smooth_ref[...], pair).astype(stage.dtype)
            for n, peer in enumerate(peers):
                off = first + n
                part = got[:, n * contrib : (n + 1) * contrib]
                if off == n_strip:
                    grouped[s_me, c] = part
                    continue
                stage[c, off] = part
                copy = pltpu.make_async_remote_copy(
                    src_ref=stage.at[c, off],
                    dst_ref=grouped.at[s_me, c],
                    send_sem=strip_send.at[c, off],
                    recv_sem=strip_recv.at[c, off],
                    device_id={"strip": peer},
                    device_id_type=MESH,
                )
                copy.start()
                strip_copies.append(copy)

    turned[:, r_blocks] = jnp.zeros((corr,) + turned.shape[2:], turned.dtype)
    turned[:, :, q_blocks] = jnp.zeros((corr, r_blocks + 1, ALIGN, LANES), turned.dtype)
    offset_load.wait()
    row_places = lax.broadcasted_iota(jnp.int32, (WIDE, vis), 0)
    col_places = lax.broadcasted_iota(jnp.int32, (TALL, vis), 0)
    factor = -0.5 / (KERNEL_WIDTH * KERNEL_WIDTH)

    def weights(spots, offset):
        delta = spots.astype(jnp.float32) - offset
        inside = (spots >= 0) & (spots < TILE)
        return jnp.where(inside, jnp.exp(factor * (delta * delta)), 0.0)

    def corner(k):
        r, q = corner_ref[0, k], corner_ref[1, k]
        rb = jnp.clip(lax.div(r, LANES), 0, r_blocks - 1)
        qb = jnp.clip(lax.div(q, ALIGN), 0, q_blocks - 2)
        return r - rb * LANES, q - qb * ALIGN, rb, qb

    def one_weight(k, carry):
        r_in, q_in, _, _ = corner(k)
        here = offsets[k]
        row_weights[k] = weights(row_places - r_in, here[0:1]).astype(row_weights.dtype)
        col_weights[k] = weights(col_places - q_in, here[1:2])
        return carry

    lax.fori_loop(0, blocks, one_weight, 0, unroll=2)
    frows_load.wait()
    fcols_load.wait()
    row_mats[...] = jnp.concatenate([frows[f] for f in range(n_facet)], axis=1)
    for load in row_loads:
        load.wait()

    facet_copies = []

    def contribute(c):
        for copy in strip_copies[c * (n_strip - 1) : (c + 1) * (n_strip - 1)]:
            copy.wait()
        flipped = []
        for x in range(n_strip):
            top, bottom = grouped[x, c, width : 2 * width], grouped[x, c, rows : rows + width]
            if x > 0:
                top = plus(top, grouped[x - 1, c, rows + width : rows + 2 * width])
            if x < n_strip - 1:
                bottom = plus(bottom, grouped[x + 1, c, 0:width])
            block = jnp.concatenate([top, grouped[x, c, 2 * width : rows], bottom], axis=0)
            flipped.append(block.T)
        flipped = jnp.concatenate(flipped, axis=1)
        for first in range(1, n_facet + 1, 2):
            peers = [lax.rem(f_me + off, n_facet) for off in (first, first + 1)]
            pair = jnp.concatenate([row_taper[position_of(row_perm, peer)] for peer in peers], axis=1)
            got = mm(flipped, pair).astype(stage2.dtype)
            for n, peer in enumerate(peers):
                off = first + n
                part = got[:, n * contrib : (n + 1) * contrib]
                if off == n_facet:
                    mine[f_me, c] = part
                    continue
                stage2[c, off] = part
                copy = pltpu.make_async_remote_copy(
                    src_ref=stage2.at[c, off],
                    dst_ref=mine.at[f_me, c],
                    send_sem=facet_send.at[c, off],
                    recv_sem=facet_recv.at[c, off],
                    device_id={"facet": peer},
                    device_id_type=MESH,
                )
                copy.start()
                facet_copies.append(copy)

    def degrid(c):
        for copy in facet_copies[c * (n_facet - 1) : (c + 1) * (n_facet - 1)]:
            copy.wait()
        for f in range(n_facet):
            spread[c, :, f * contrib : (f + 1) * contrib] = mm(fcols[f], mine[f, c]).astype(spread.dtype)
        for rb in range(r_blocks):
            turned[c, rb, 0:q_blocks] = (
                lax.dot_general(
                    spread[c],
                    row_mats[rb * LANES : (rb + 1) * LANES],
                    ACROSS,
                    preferred_element_type=jnp.float32,
                )
                .astype(turned.dtype)
                .reshape(q_blocks, ALIGN, LANES)
            )

        def one_block(k, carry):
            _, _, rb, qb = corner(k)
            tile = jnp.concatenate(
                [
                    jnp.concatenate([turned[c, rb + j, qb + i] for j in range(2)], axis=1)
                    for i in range(TALL // ALIGN)
                ],
                axis=0,
            )
            along = mm(tile[:, :WIDE], row_weights[k])
            values[pl.ds(c * blocks + k, 1), :] = jnp.sum(along * col_weights[k], axis=0, keepdims=True)
            return carry

        lax.fori_loop(0, blocks, one_block, 0, unroll=8)

    contribute(0)
    for c in range(corr):
        if c + 1 < corr:
            degrid(c)
            contribute(c + 1)
            continue
        index_load.wait()
        for n in range(corr):
            row = gains_ref[n : n + 1, :]
            product[n] = looked_up(row, index[:, 0, :]) * looked_up(row, index[:, 1, :])
        dest = dest_ref[...]
        k_row = lax.broadcasted_iota(jnp.int32, (blocks, blocks), 0)
        k_col = lax.broadcasted_iota(jnp.int32, (blocks, blocks), 1)
        dest_wide = jnp.broadcast_to(dest, (blocks, blocks))
        dest_tall = jnp.sum(jnp.where(k_row == k_col, dest_wide, 0), axis=1, keepdims=True)
        same = (dest_tall == dest_wide) & (k_row < k_col)
        rank = jnp.sum(jnp.where(same, 1, 0), axis=0, keepdims=True)
        target = dest * capacity + rank
        code = jnp.concatenate([target * corr + n for n in range(corr)], axis=1)
        places = lax.broadcasted_iota(jnp.int32, onehot.shape, 0)
        onehot[...] = jnp.where(places == code, 1.0, 0.0).astype(onehot.dtype)
        degrid(c)

    outgoing[...] = (
        mm(onehot[...], values[...].astype(jnp.bfloat16))
        .astype(outgoing.dtype)
        .reshape(outgoing.shape)
    )
    pl.semaphore_wait(ready_sem, n_strip - 1)

    vis_copies = []
    for f_off in [n_facet // 2] + [n for n in range(n_facet) if n != n_facet // 2]:
        f_peer = lax.rem(f_me + f_off, n_facet)
        for s_off in range(n_strip):
            if f_off == 0 and s_off == 0:
                continue
            s_peer = lax.rem(s_me + s_off, n_strip)
            off = f_off * n_strip + s_off
            copy = pltpu.make_async_remote_copy(
                src_ref=outgoing.at[f_peer * n_strip + s_peer],
                dst_ref=arrived.at[me],
                send_sem=vis_send.at[off],
                recv_sem=vis_recv.at[off],
                device_id={"facet": f_peer, "strip": s_peer},
                device_id_type=MESH,
            )
            copy.start()
            vis_copies.append(copy)
    arrived[me] = outgoing[me]
    subgrid_copies = []
    for c in range(corr):
        subgrid[c] = lax.dot_general(
            row_mats[...], spread[c], ACROSS, preferred_element_type=jnp.float32
        ).astype(subgrid.dtype)
        copy = pltpu.make_async_copy(subgrid.at[c], subgrid_out.at[c], out_sem.at[c])
        copy.start()
        subgrid_copies.append(copy)
    observed_load.wait()

    for copy in vis_copies:
        copy.wait()
    wide[...] = arrived[...].astype(jnp.float32).reshape(wide.shape)
    for c in range(corr):
        placed = wide[pl.ds(c, devices * capacity, stride=corr), :]
        residual_out[:, c, :] = observed[:, c, :] - product[c] * placed
    for copy in subgrid_copies:
        copy.wait()


def pass_kernel(a_ref, b_ref, a_out, b_out, a_buf, b_buf, in_sem, out_sem):
    parts = a_ref.shape[0]
    pairs = [(a_ref.at[n], a_buf.at[n], a_out.at[n]) for n in range(parts)]
    pairs.append((b_ref, b_buf, b_out))
    loads = [pltpu.make_async_copy(src, buf, in_sem.at[n]) for n, (src, buf, _) in enumerate(pairs)]
    stores = [pltpu.make_async_copy(buf, dst, out_sem.at[n]) for n, (_, buf, dst) in enumerate(pairs)]
    for load in loads:
        load.start()
    for load, store in zip(loads, stores):
        load.wait()
        store.start()
    for store in stores:
        store.wait()


def handed_on(subgrid, residual):
    parts = 8
    cut = subgrid.reshape(parts, -1, subgrid.shape[-1])
    remote = pl.BlockSpec(memory_space=pl.ANY)
    a, b = pl.pallas_call(
        pass_kernel,
        in_specs=[remote, remote],
        out_specs=[remote, remote],
        out_shape=[
            jax.ShapeDtypeStruct(cut.shape, cut.dtype),
            jax.ShapeDtypeStruct(residual.shape, residual.dtype),
        ],
        scratch_shapes=[
            pltpu.VMEM(cut.shape, cut.dtype),
            pltpu.VMEM(residual.shape, residual.dtype),
            pltpu.SemaphoreType.DMA((parts + 1,)),
            pltpu.SemaphoreType.DMA((parts + 1,)),
        ],
        name="handed_on",
    )(cut, residual)
    return a.reshape(subgrid.shape), b


def on_device(
    sky_components,
    scale_kernels,
    row_taper,
    col_taper,
    finish_rows,
    finish_cols,
    subgrid_owner,
    block_cell,
    vis_offset,
    block_owner,
    observed,
    antenna_pair_index,
    gains,
):
    n_facet = lax.axis_size("facet")
    n_strip = lax.axis_size("strip")
    devices = n_facet * n_strip
    comp = sky_components[0]
    corr, scales, rows, side = comp.shape
    tall = rows + scale_kernels.shape[1] - 1
    sub_side, contrib = finish_cols.shape[1], finish_cols.shape[2]
    blocks, _, vis = vis_offset.shape
    sub_rows, sub_cols = row_taper.shape[2] // contrib, col_taper.shape[2] // contrib
    slots = observed.shape[0]
    per_device = slots // devices * corr
    whole = pl.BlockSpec(memory_space=pltpu.VMEM)
    scalars = pl.BlockSpec(memory_space=pltpu.SMEM)
    remote = pl.BlockSpec(memory_space=pl.ANY)
    bf16, f32 = jnp.bfloat16, jnp.float32
    dma = pltpu.SemaphoreType.DMA
    subgrid, residual = pl.pallas_call(
        functools.partial(whole_kernel, n_facet, n_strip),
        in_specs=[scalars, scalars, whole, whole, whole] + [remote] * 8,
        out_specs=[remote, whole],
        out_shape=[
            jax.ShapeDtypeStruct((corr, sub_side, sub_side), bf16),
            jax.ShapeDtypeStruct(observed.shape, f32),
        ],
        scratch_shapes=[
            pltpu.VMEM((corr, scales, rows, side), bf16),
            pltpu.VMEM((sub_cols, side, contrib), bf16),
            pltpu.VMEM((sub_rows, side, contrib), bf16),
            pltpu.VMEM(finish_rows.shape, bf16),
            pltpu.VMEM(finish_cols.shape, bf16),
            pltpu.VMEM(vis_offset.shape, f32),
            pltpu.VMEM(antenna_pair_index.shape, jnp.int32),
            pltpu.VMEM(observed.shape, f32),
            pltpu.VMEM((scales, 2 * LANES), f32),
            pltpu.VMEM((scales, tall, rows), bf16),
            pltpu.VMEM((scales, COL_TILE + 2 * LANES, COL_TILE), bf16),
            pltpu.VMEM((scales, tall, side + 2 * LANES), bf16),
            pltpu.VMEM((tall, side), bf16),
            pltpu.VMEM((corr, n_strip, tall, contrib), bf16),
            pltpu.VMEM((n_strip, corr, tall, contrib), bf16),
            pltpu.VMEM((corr, n_facet, contrib, contrib), bf16),
            pltpu.VMEM((n_facet, corr, contrib, contrib), bf16),
            pltpu.VMEM((sub_side, n_facet * contrib), bf16),
            pltpu.VMEM((corr, sub_side, n_facet * contrib), bf16),
            pltpu.VMEM((corr, sub_side // LANES + 1, sub_side // ALIGN + 1, ALIGN, LANES), bf16),
            pltpu.VMEM((corr, sub_side, sub_side), bf16),
            pltpu.VMEM((blocks, WIDE, vis), bf16),
            pltpu.VMEM((blocks, TALL, vis), f32),
            pltpu.VMEM((devices * per_device, corr * blocks), bf16),
            pltpu.VMEM((corr * blocks, vis), f32),
            pltpu.VMEM((devices, per_device, vis), bf16),
            pltpu.VMEM((devices, per_device, vis), bf16),
            pltpu.VMEM((devices * per_device, vis), f32),
            pltpu.VMEM((corr, slots, vis), f32),
            dma((corr + 5 + sub_cols + sub_rows,)),
            dma((corr, n_strip)),
            dma((corr, n_strip)),
            dma((corr, n_facet)),
            dma((corr, n_facet)),
            dma((devices,)),
            dma((devices,)),
            dma((corr,)),
            pltpu.SemaphoreType.REGULAR,
        ],
        compiler_params=pltpu.CompilerParams(
            collective_id=0, has_side_effects=True, vmem_limit_bytes=60 * 1024 * 1024
        ),
        name="sky_to_residual",
    )(
        subgrid_owner,
        block_cell.T,
        scale_kernels,
        block_owner.reshape(1, blocks),
        gains,
        comp,
        col_taper[0],
        row_taper[0],
        finish_rows,
        finish_cols,
        vis_offset,
        antenna_pair_index,
        observed,
    )
    subgrid, residual = handed_on(subgrid, residual)
    return subgrid[None], residual


def solution(mesh):
    placed = (
        P("facet", None, None, "strip", None),
        P(),
        P("facet", None, None),
        P("facet", None, None),
        P(),
        P(),
        P(),
        P(("facet", "strip"), None),
        P(("facet", "strip"), None, None),
        P(("facet", "strip"), None),
        P(("facet", "strip"), None, None),
        P(("facet", "strip"), None, None),
        P(),
    )
    return jax.shard_map(
        on_device,
        mesh=mesh,
        in_specs=placed,
        out_specs=(P(("facet", "strip"), None, None, None), P(("facet", "strip"), None, None)),
        check_vma=False,
    )
```

```python
import functools

import jax
import jax.numpy as jnp
from jax import lax
from jax.experimental import pallas as pl
from jax.experimental.pallas import tpu as pltpu
from jax.sharding import PartitionSpec as P

TILE = 32
KERNEL_WIDTH = 1.5
LANES = 128
COL_TILE = 256
ALIGN = 16
TALL = TILE + ALIGN
WIDE = LANES + TILE
MESH = pl.DeviceIdType.MESH
ACROSS = (((1,), (1,)), ((), ()))


def mm(a, b):
    return jnp.dot(a, b, preferred_element_type=jnp.float32)


def row_chunks(rows, width):
    count = rows // LANES
    chunks = []
    for h in range(count):
        low = h * LANES if h else -width
        high = (h + 1) * LANES if h < count - 1 else rows + width
        chunks.append((low, high, max(0, low - width), min(rows, high + width)))
    return chunks


def fill_bands(taps_ref, pad_ref, across_ref, down_ref, width, chunks):
    scales, taps = taps_ref.shape
    span = LANES + taps - 1
    pad_ref[...] = jnp.zeros_like(pad_ref)
    pad_ref[:, 0:taps] = taps_ref[...]
    down_ref[...] = jnp.zeros_like(down_ref)
    for s in range(scales):
        row = jnp.broadcast_to(pad_ref[s : s + 1, :], (LANES, 2 * LANES))
        band = pltpu.roll(row, 0, 1, stride=1, stride_axis=0)
        down = band.T[:span].astype(down_ref.dtype)
        for tile in range(COL_TILE // LANES):
            start = LANES - width + tile * LANES
            down_ref[s, start : start + span, tile * LANES : (tile + 1) * LANES] = down
        for h, (low, high, x_low, x_high) in enumerate(chunks):
            for first in range(0, high - low, LANES):
                size = min(LANES, high - low - first)
                line = jnp.broadcast_to(pad_ref[s : s + 1, :], (size, 2 * LANES))
                shift = (low - width - x_low + first) % (2 * LANES)
                if shift:
                    line = pltpu.roll(line, shift, 1)
                line = pltpu.roll(line, 0, 1, stride=1, stride_axis=0)
                across_ref[h, s, first : first + size] = line[:, 0 : x_high - x_low].astype(
                    across_ref.dtype
                )


def plus(a, b):
    return (a.astype(jnp.float32) + b.astype(jnp.float32)).astype(a.dtype)


def position_of(values, wanted):
    place = 0
    for j, value in enumerate(values):
        gap = value - wanted
        place += j * jnp.maximum(1 - gap * gap, 0)
    return jnp.minimum(place, len(values) - 1)


def looked_up(row, index):
    low, high = index % LANES, index // LANES
    out = None
    for chunk in range(row.shape[1] // LANES):
        table = jnp.broadcast_to(row[:, chunk * LANES : (chunk + 1) * LANES], index.shape)
        got = jnp.take_along_axis(table, low, axis=1, mode="promise_in_bounds")
        out = got if out is None else jnp.where(high == chunk, got, out)
    return out


def whole_kernel(
    n_facet,
    n_strip,
    owner_ref,
    corner_ref,
    taps_ref,
    dest_ref,
    gains_ref,
    x_ref,
    col_in,
    row_in,
    frows_in,
    fcols_in,
    offset_in,
    index_in,
    observed_in,
    subgrid_out,
    residual_out,
    x_buf,
    col_taper,
    row_taper,
    frows,
    fcols,
    offsets,
    index,
    observed,
    pad_ref,
    across_ref,
    down_ref,
    y_ref,
    smooth_ref,
    stage,
    grouped,
    stage2,
    mine,
    row_mats,
    spread,
    turned,
    subgrid,
    row_weights,
    col_weights,
    onehot,
    values,
    outgoing,
    arrived,
    wide,
    product,
    load_sem,
    strip_send,
    strip_recv,
    facet_send,
    facet_recv,
    vis_send,
    vis_recv,
    out_sem,
    ready_sem,
):
    corr, scales, rows, side = x_ref.shape
    width = (taps_ref.shape[1] - 1) // 2
    chunks = row_chunks(rows, width)
    n_chunk = len(chunks)
    tall = chunks[0][1] - chunks[0][0]
    tiles = side // COL_TILE
    contrib = fcols.shape[2]
    sub_side = fcols.shape[1]
    blocks = offsets.shape[0]
    vis = offsets.shape[2]
    devices = n_facet * n_strip
    capacity = observed.shape[0] // devices
    sub_cols = col_taper.shape[0]
    sub_rows = row_taper.shape[0]
    r_blocks, q_blocks = sub_side // LANES, sub_side // ALIGN
    f_me = lax.axis_index("facet")
    s_me = lax.axis_index("strip")
    me = f_me * n_strip + s_me

    x_loads = []
    for c in range(corr):
        x_low = 0
        for h, (_, _, _, x_high) in enumerate(chunks):
            part = pl.ds(x_low, x_high - x_low)
            x_loads.append(
                pltpu.make_async_copy(
                    x_ref.at[c, :, part], x_buf.at[c, :, part], load_sem.at[c * n_chunk + h]
                )
            )
            x_low = x_high
    others = [
        pltpu.make_async_copy(src, dst, load_sem.at[corr * n_chunk + n])
        for n, (src, dst) in enumerate(
            (
                (index_in, index),
                (offset_in, offsets),
                (frows_in, frows),
                (fcols_in, fcols),
                (observed_in, observed),
            )
        )
    ]
    index_load, offset_load, frows_load, fcols_load, observed_load = others
    col_loads = [
        pltpu.make_async_copy(
            col_in.at[:, pl.ds(b * contrib, contrib)], col_taper.at[b], load_sem.at[corr * n_chunk + 5 + b]
        )
        for b in range(sub_cols)
    ]
    row_loads = [
        pltpu.make_async_copy(
            row_in.at[:, pl.ds(a * contrib, contrib)],
            row_taper.at[a],
            load_sem.at[corr * n_chunk + 5 + sub_cols + a],
        )
        for a in range(sub_rows)
    ]
    for load in x_loads[:n_chunk] + col_loads + x_loads[n_chunk:] + others + row_loads:
        load.start()

    barrier = pltpu.get_barrier_semaphore()
    for off in range(1, n_strip):
        pl.semaphore_signal(
            barrier, inc=1, device_id={"strip": lax.rem(s_me + off, n_strip)}, device_id_type=MESH
        )
    for off in range(1, n_facet):
        pl.semaphore_signal(
            barrier, inc=1, device_id={"facet": lax.rem(f_me + off, n_facet)}, device_id_type=MESH
        )
    fill_bands(taps_ref, pad_ref, across_ref, down_ref, width, chunks)
    y_ref[:, :, 0:LANES] = jnp.zeros((scales, tall, LANES), y_ref.dtype)
    y_ref[:, :, LANES + side : 2 * LANES + side] = jnp.zeros((scales, tall, LANES), y_ref.dtype)
    col_perm = [lax.rem(owner_ref[b], n_strip) for b in range(sub_cols)]
    row_perm = [lax.div(owner_ref[a * sub_cols], n_strip) for a in range(sub_rows)]

    strip_copies = []
    for n_part in range(corr * n_chunk):
        c, h = divmod(n_part, n_chunk)
        low, high, x_low, x_high = chunks[h]
        x_loads[n_part].wait()
        for s in range(scales):
            for n in range(0, side, COL_TILE):
                y_ref[s, :, LANES + n : LANES + n + COL_TILE] = mm(
                    across_ref[h, s], x_buf[c, s, x_low:x_high, n : n + COL_TILE]
                ).astype(y_ref.dtype)

        def one_tile(tile, carry):
            first = pl.multiple_of(tile * COL_TILE, COL_TILE)
            smoothed = jnp.zeros((tall, COL_TILE), jnp.float32)
            for s in range(scales):
                smoothed += mm(y_ref[s, :, pl.ds(first, COL_TILE + 2 * LANES)], down_ref[s])
            smooth_ref[:, pl.ds(first, COL_TILE)] = smoothed.astype(smooth_ref.dtype)
            return carry

        lax.fori_loop(0, tiles, one_tile, 0, unroll=4)
        if n_part == 0:
            for load in col_loads:
                load.wait()
            pl.semaphore_wait(barrier, n_strip + n_facet - 2)
            for off in range(1, n_strip):
                pl.semaphore_signal(
                    ready_sem,
                    inc=1,
                    device_id={"strip": lax.rem(s_me + off, n_strip)},
                    device_id_type=MESH,
                )
        for first in range(1, n_strip + 1, 2):
            peers = [lax.rem(s_me + off, n_strip) for off in (first, first + 1)]
            pair = jnp.concatenate([col_taper[position_of(col_perm, peer)] for peer in peers], axis=1)
            got = mm(smooth_ref[...], pair).astype(stage.dtype)
            for n, peer in enumerate(peers):
                off = first + n
                part = got[:, n * contrib : (n + 1) * contrib]
                if off == n_strip:
                    grouped[s_me, n_part] = part
                    continue
                stage[n_part, off] = part
                copy = pltpu.make_async_remote_copy(
                    src_ref=stage.at[n_part, off],
                    dst_ref=grouped.at[s_me, n_part],
                    send_sem=strip_send.at[n_part, off],
                    recv_sem=strip_recv.at[n_part, off],
                    device_id={"strip": peer},
                    device_id_type=MESH,
                )
                copy.start()
                strip_copies.append(copy)

    turned[:, r_blocks] = jnp.zeros((corr,) + turned.shape[2:], turned.dtype)
    turned[:, :, q_blocks] = jnp.zeros((corr, r_blocks + 1, ALIGN, LANES), turned.dtype)
    offset_load.wait()
    row_places = lax.broadcasted_iota(jnp.int32, (WIDE, vis), 0)
    col_places = lax.broadcasted_iota(jnp.int32, (TALL, vis), 0)
    factor = -0.5 / (KERNEL_WIDTH * KERNEL_WIDTH)

    def weights(spots, offset):
        delta = spots.astype(jnp.float32) - offset
        inside = (spots >= 0) & (spots < TILE)
        return jnp.where(inside, jnp.exp(factor * (delta * delta)), 0.0)

    def corner(k):
        r, q = corner_ref[0, k], corner_ref[1, k]
        rb = jnp.clip(lax.div(r, LANES), 0, r_blocks - 1)
        qb = jnp.clip(lax.div(q, ALIGN), 0, q_blocks - 2)
        return r - rb * LANES, q - qb * ALIGN, rb, qb

    def one_weight(k, carry):
        r_in, q_in, _, _ = corner(k)
        here = offsets[k]
        row_weights[k] = weights(row_places - r_in, here[0:1]).astype(row_weights.dtype)
        col_weights[k] = weights(col_places - q_in, here[1:2])
        return carry

    lax.fori_loop(0, blocks, one_weight, 0, unroll=2)
    frows_load.wait()
    fcols_load.wait()
    row_mats[...] = jnp.concatenate([frows[f] for f in range(n_facet)], axis=1)
    for load in row_loads:
        load.wait()

    facet_copies = []

    def contribute(c):
        each = n_chunk * (n_strip - 1)
        for copy in strip_copies[c * each : (c + 1) * each]:
            copy.wait()
        head, tail = c * n_chunk, (c + 1) * n_chunk - 1
        flipped = []
        for x in range(n_strip):
            top = grouped[x, head, width : 2 * width]
            bottom = grouped[x, tail, tall - 2 * width : tall - width]
            if x > 0:
                top = plus(top, grouped[x - 1, tail, tall - width : tall])
            if x < n_strip - 1:
                bottom = plus(bottom, grouped[x + 1, head, 0:width])
            middle = []
            for n_part in range(head, tail + 1):
                start = 2 * width if n_part == head else 0
                stop = tall - 2 * width if n_part == tail else tall
                middle.append(grouped[x, n_part, start:stop])
            block = jnp.concatenate([top] + middle + [bottom], axis=0)
            flipped.append(block.T)
        flipped = jnp.concatenate(flipped, axis=1)
        for first in range(1, n_facet + 1, 2):
            peers = [lax.rem(f_me + off, n_facet) for off in (first, first + 1)]
            pair = jnp.concatenate([row_taper[position_of(row_perm, peer)] for peer in peers], axis=1)
            got = mm(flipped, pair).astype(stage2.dtype)
            for n, peer in enumerate(peers):
                off = first + n
                part = got[:, n * contrib : (n + 1) * contrib]
                if off == n_facet:
                    mine[f_me, c] = part
                    continue
                stage2[c, off] = part
                copy = pltpu.make_async_remote_copy(
                    src_ref=stage2.at[c, off],
                    dst_ref=mine.at[f_me, c],
                    send_sem=facet_send.at[c, off],
                    recv_sem=facet_recv.at[c, off],
                    device_id={"facet": peer},
                    device_id_type=MESH,
                )
                copy.start()
                facet_copies.append(copy)

    def degrid(c):
        for copy in facet_copies[c * (n_facet - 1) : (c + 1) * (n_facet - 1)]:
            copy.wait()
        for f in range(n_facet):
            spread[c, :, f * contrib : (f + 1) * contrib] = mm(fcols[f], mine[f, c]).astype(spread.dtype)
        for rb in range(r_blocks):
            turned[c, rb, 0:q_blocks] = (
                lax.dot_general(
                    spread[c],
                    row_mats[rb * LANES : (rb + 1) * LANES],
                    ACROSS,
                    preferred_element_type=jnp.float32,
                )
                .astype(turned.dtype)
                .reshape(q_blocks, ALIGN, LANES)
            )

        def one_block(k, carry):
            _, _, rb, qb = corner(k)
            tile = jnp.concatenate(
                [
                    jnp.concatenate([turned[c, rb + j, qb + i] for j in range(2)], axis=1)
                    for i in range(TALL // ALIGN)
                ],
                axis=0,
            )
            along = mm(tile[:, :WIDE], row_weights[k])
            values[pl.ds(c * blocks + k, 1), :] = jnp.sum(along * col_weights[k], axis=0, keepdims=True)
            return carry

        lax.fori_loop(0, blocks, one_block, 0, unroll=8)

    contribute(0)
    index_load.wait()
    for n in range(corr):
        row = gains_ref[n : n + 1, :]
        product[n] = looked_up(row, index[:, 0, :]) * looked_up(row, index[:, 1, :])
    dest = dest_ref[...]
    k_row = lax.broadcasted_iota(jnp.int32, (blocks, blocks), 0)
    k_col = lax.broadcasted_iota(jnp.int32, (blocks, blocks), 1)
    dest_wide = jnp.broadcast_to(dest, (blocks, blocks))
    dest_tall = jnp.sum(jnp.where(k_row == k_col, dest_wide, 0), axis=1, keepdims=True)
    same = (dest_tall == dest_wide) & (k_row < k_col)
    rank = jnp.sum(jnp.where(same, 1, 0), axis=0, keepdims=True)
    target = dest * capacity + rank
    code = jnp.concatenate([target * corr + n for n in range(corr)], axis=1)
    places = lax.broadcasted_iota(jnp.int32, onehot.shape, 0)
    onehot[...] = jnp.where(places == code, 1.0, 0.0).astype(onehot.dtype)
    for c in range(1, corr):
        contribute(c)
        degrid(c - 1)
    degrid(corr - 1)

    outgoing[...] = (
        mm(onehot[...], values[...].astype(jnp.bfloat16))
        .astype(outgoing.dtype)
        .reshape(outgoing.shape)
    )
    pl.semaphore_wait(ready_sem, n_strip - 1)

    vis_copies = []
    for f_off in [n_facet // 2] + [n for n in range(n_facet) if n != n_facet // 2]:
        f_peer = lax.rem(f_me + f_off, n_facet)
        for s_off in range(n_strip):
            if f_off == 0 and s_off == 0:
                continue
            s_peer = lax.rem(s_me + s_off, n_strip)
            off = f_off * n_strip + s_off
            copy = pltpu.make_async_remote_copy(
                src_ref=outgoing.at[f_peer * n_strip + s_peer],
                dst_ref=arrived.at[me],
                send_sem=vis_send.at[off],
                recv_sem=vis_recv.at[off],
                device_id={"facet": f_peer, "strip": s_peer},
                device_id_type=MESH,
            )
            copy.start()
            vis_copies.append(copy)
    arrived[me] = outgoing[me]
    subgrid_copies = []
    for c in range(corr):
        subgrid[c] = lax.dot_general(
            row_mats[...], spread[c], ACROSS, preferred_element_type=jnp.float32
        ).astype(subgrid.dtype)
        copy = pltpu.make_async_copy(subgrid.at[c], subgrid_out.at[c], out_sem.at[c])
        copy.start()
        subgrid_copies.append(copy)
    observed_load.wait()

    for copy in vis_copies:
        copy.wait()
    wide[...] = arrived[...].astype(jnp.float32).reshape(wide.shape)
    for c in range(corr):
        placed = wide[pl.ds(c, devices * capacity, stride=corr), :]
        residual_out[:, c, :] = observed[:, c, :] - product[c] * placed
    for copy in subgrid_copies:
        copy.wait()


def pass_kernel(a_ref, b_ref, a_out, b_out, a_buf, b_buf, in_sem, out_sem):
    parts = a_ref.shape[0]
    pairs = [(a_ref.at[n], a_buf.at[n], a_out.at[n]) for n in range(parts)]
    pairs.append((b_ref, b_buf, b_out))
    loads = [pltpu.make_async_copy(src, buf, in_sem.at[n]) for n, (src, buf, _) in enumerate(pairs)]
    stores = [pltpu.make_async_copy(buf, dst, out_sem.at[n]) for n, (_, buf, dst) in enumerate(pairs)]
    for load in loads:
        load.start()
    for load, store in zip(loads, stores):
        load.wait()
        store.start()
    for store in stores:
        store.wait()


def handed_on(subgrid, residual):
    parts = 8
    cut = subgrid.reshape(parts, -1, subgrid.shape[-1])
    remote = pl.BlockSpec(memory_space=pl.ANY)
    a, b = pl.pallas_call(
        pass_kernel,
        in_specs=[remote, remote],
        out_specs=[remote, remote],
        out_shape=[
            jax.ShapeDtypeStruct(cut.shape, cut.dtype),
            jax.ShapeDtypeStruct(residual.shape, residual.dtype),
        ],
        scratch_shapes=[
            pltpu.VMEM(cut.shape, cut.dtype),
            pltpu.VMEM(residual.shape, residual.dtype),
            pltpu.SemaphoreType.DMA((parts + 1,)),
            pltpu.SemaphoreType.DMA((parts + 1,)),
        ],
        name="handed_on",
    )(cut, residual)
    return a.reshape(subgrid.shape), b


def on_device(
    sky_components,
    scale_kernels,
    row_taper,
    col_taper,
    finish_rows,
    finish_cols,
    subgrid_owner,
    block_cell,
    vis_offset,
    block_owner,
    observed,
    antenna_pair_index,
    gains,
):
    n_facet = lax.axis_size("facet")
    n_strip = lax.axis_size("strip")
    devices = n_facet * n_strip
    comp = sky_components[0]
    corr, scales, rows, side = comp.shape
    chunks = row_chunks(rows, (scale_kernels.shape[1] - 1) // 2)
    n_chunk = len(chunks)
    tall = chunks[0][1] - chunks[0][0]
    sub_side, contrib = finish_cols.shape[1], finish_cols.shape[2]
    blocks, _, vis = vis_offset.shape
    sub_rows, sub_cols = row_taper.shape[2] // contrib, col_taper.shape[2] // contrib
    slots = observed.shape[0]
    per_device = slots // devices * corr
    whole = pl.BlockSpec(memory_space=pltpu.VMEM)
    scalars = pl.BlockSpec(memory_space=pltpu.SMEM)
    remote = pl.BlockSpec(memory_space=pl.ANY)
    bf16, f32 = jnp.bfloat16, jnp.float32
    dma = pltpu.SemaphoreType.DMA
    subgrid, residual = pl.pallas_call(
        functools.partial(whole_kernel, n_facet, n_strip),
        in_specs=[scalars, scalars, whole, whole, whole] + [remote] * 8,
        out_specs=[remote, whole],
        out_shape=[
            jax.ShapeDtypeStruct((corr, sub_side, sub_side), bf16),
            jax.ShapeDtypeStruct(observed.shape, f32),
        ],
        scratch_shapes=[
            pltpu.VMEM((corr, scales, rows, side), bf16),
            pltpu.VMEM((sub_cols, side, contrib), bf16),
            pltpu.VMEM((sub_rows, side, contrib), bf16),
            pltpu.VMEM(finish_rows.shape, bf16),
            pltpu.VMEM(finish_cols.shape, bf16),
            pltpu.VMEM(vis_offset.shape, f32),
            pltpu.VMEM(antenna_pair_index.shape, jnp.int32),
            pltpu.VMEM(observed.shape, f32),
            pltpu.VMEM((scales, 2 * LANES), f32),
            pltpu.VMEM((n_chunk, scales, tall, chunks[0][3] - chunks[0][2]), bf16),
            pltpu.VMEM((scales, COL_TILE + 2 * LANES, COL_TILE), bf16),
            pltpu.VMEM((scales, tall, side + 2 * LANES), bf16),
            pltpu.VMEM((tall, side), bf16),
            pltpu.VMEM((corr * n_chunk, n_strip, tall, contrib), bf16),
            pltpu.VMEM((n_strip, corr * n_chunk, tall, contrib), bf16),
            pltpu.VMEM((corr, n_facet, contrib, contrib), bf16),
            pltpu.VMEM((n_facet, corr, contrib, contrib), bf16),
            pltpu.VMEM((sub_side, n_facet * contrib), bf16),
            pltpu.VMEM((corr, sub_side, n_facet * contrib), bf16),
            pltpu.VMEM((corr, sub_side // LANES + 1, sub_side // ALIGN + 1, ALIGN, LANES), bf16),
            pltpu.VMEM((corr, sub_side, sub_side), bf16),
            pltpu.VMEM((blocks, WIDE, vis), bf16),
            pltpu.VMEM((blocks, TALL, vis), f32),
            pltpu.VMEM((devices * per_device, corr * blocks), bf16),
            pltpu.VMEM((corr * blocks, vis), f32),
            pltpu.VMEM((devices, per_device, vis), bf16),
            pltpu.VMEM((devices, per_device, vis), bf16),
            pltpu.VMEM((devices * per_device, vis), f32),
            pltpu.VMEM((corr, slots, vis), f32),
            dma((corr * n_chunk + 5 + sub_cols + sub_rows,)),
            dma((corr * n_chunk, n_strip)),
            dma((corr * n_chunk, n_strip)),
            dma((corr, n_facet)),
            dma((corr, n_facet)),
            dma((devices,)),
            dma((devices,)),
            dma((corr,)),
            pltpu.SemaphoreType.REGULAR,
        ],
        compiler_params=pltpu.CompilerParams(
            collective_id=0, has_side_effects=True, vmem_limit_bytes=60 * 1024 * 1024
        ),
        name="sky_to_residual",
    )(
        subgrid_owner,
        block_cell.T,
        scale_kernels,
        block_owner.reshape(1, blocks),
        gains,
        comp,
        col_taper[0],
        row_taper[0],
        finish_rows,
        finish_cols,
        vis_offset,
        antenna_pair_index,
        observed,
    )
    subgrid, residual = handed_on(subgrid, residual)
    return subgrid[None], residual


def solution(mesh):
    placed = (
        P("facet", None, None, "strip", None),
        P(),
        P("facet", None, None),
        P("facet", None, None),
        P(),
        P(),
        P(),
        P(("facet", "strip"), None),
        P(("facet", "strip"), None, None),
        P(("facet", "strip"), None),
        P(("facet", "strip"), None, None),
        P(("facet", "strip"), None, None),
        P(),
    )
    return jax.shard_map(
        on_device,
        mesh=mesh,
        in_specs=placed,
        out_specs=(P(("facet", "strip"), None, None, None), P(("facet", "strip"), None, None)),
        check_vma=False,
    )
```

```python
import functools

import jax
import jax.numpy as jnp
from jax import lax
from jax.experimental import pallas as pl
from jax.experimental.pallas import tpu as pltpu
from jax.sharding import PartitionSpec as P

TILE = 32
KERNEL_WIDTH = 1.5
LANES = 128
COL_TILE = 256
ALIGN = 16
TALL = TILE + ALIGN
WIDE = LANES + TILE
MESH = pl.DeviceIdType.MESH
ACROSS = (((1,), (1,)), ((), ()))


def mm(a, b):
    return jnp.dot(a, b, preferred_element_type=jnp.float32)


def row_chunks(rows, width):
    count = rows // LANES
    chunks = []
    for h in range(count):
        low = h * LANES if h else -width
        high = (h + 1) * LANES if h < count - 1 else rows + width
        chunks.append((low, high, max(0, low - width), min(rows, high + width)))
    return chunks


def fill_bands(taps_ref, pad_ref, across_ref, down_ref, width, chunks):
    scales, taps = taps_ref.shape
    span = LANES + taps - 1
    pad_ref[...] = jnp.zeros_like(pad_ref)
    pad_ref[:, 0:taps] = taps_ref[...]
    down_ref[...] = jnp.zeros_like(down_ref)
    for s in range(scales):
        row = jnp.broadcast_to(pad_ref[s : s + 1, :], (LANES, 2 * LANES))
        band = pltpu.roll(row, 0, 1, stride=1, stride_axis=0)
        down = band.T[:span].astype(down_ref.dtype)
        for tile in range(COL_TILE // LANES):
            start = LANES - width + tile * LANES
            down_ref[s, start : start + span, tile * LANES : (tile + 1) * LANES] = down
        for h, (low, high, x_low, x_high) in enumerate(chunks):
            for first in range(0, high - low, LANES):
                size = min(LANES, high - low - first)
                line = jnp.broadcast_to(pad_ref[s : s + 1, :], (size, 2 * LANES))
                shift = (low - width - x_low + first) % (2 * LANES)
                if shift:
                    line = pltpu.roll(line, shift, 1)
                line = pltpu.roll(line, 0, 1, stride=1, stride_axis=0)
                across_ref[h, s, first : first + size] = line[:, 0 : x_high - x_low].astype(
                    across_ref.dtype
                )


def plus(a, b):
    return (a.astype(jnp.float32) + b.astype(jnp.float32)).astype(a.dtype)


def position_of(values, wanted):
    place = 0
    for j, value in enumerate(values):
        gap = value - wanted
        place += j * jnp.maximum(1 - gap * gap, 0)
    return jnp.minimum(place, len(values) - 1)


def flipped_bits(place, mask, count):
    bit, out = 1, 0
    while bit < count:
        held = lax.rem(lax.div(place, bit), 2)
        out += bit * ((1 - held) if mask & bit else held)
        bit *= 2
    return out


def looked_up(row, index):
    low, high = index % LANES, index // LANES
    out = None
    for chunk in range(row.shape[1] // LANES):
        table = jnp.broadcast_to(row[:, chunk * LANES : (chunk + 1) * LANES], index.shape)
        got = jnp.take_along_axis(table, low, axis=1, mode="promise_in_bounds")
        out = got if out is None else jnp.where(high == chunk, got, out)
    return out


def whole_kernel(
    n_facet,
    n_strip,
    owner_ref,
    corner_ref,
    taps_ref,
    dest_ref,
    gains_ref,
    x_ref,
    col_in,
    row_in,
    frows_in,
    fcols_in,
    offset_in,
    index_in,
    observed_in,
    subgrid_out,
    residual_out,
    x_buf,
    col_taper,
    row_taper,
    frows,
    fcols,
    offsets,
    index,
    observed,
    pad_ref,
    across_ref,
    down_ref,
    y_ref,
    smooth_ref,
    stage,
    grouped,
    stage2,
    mine,
    row_mats,
    spread,
    turned,
    subgrid,
    row_weights,
    col_weights,
    onehot,
    values,
    outgoing,
    arrived,
    wide,
    product,
    load_sem,
    strip_send,
    strip_recv,
    facet_send,
    facet_recv,
    vis_send,
    vis_recv,
    out_sem,
    ready_sem,
):
    corr, scales, rows, side = x_ref.shape
    width = (taps_ref.shape[1] - 1) // 2
    chunks = row_chunks(rows, width)
    n_chunk = len(chunks)
    tall = chunks[0][1] - chunks[0][0]
    tiles = side // COL_TILE
    contrib = fcols.shape[2]
    sub_side = fcols.shape[1]
    blocks = offsets.shape[0]
    vis = offsets.shape[2]
    devices = n_facet * n_strip
    capacity = observed.shape[0] // devices
    sub_cols = col_taper.shape[0]
    sub_rows = row_taper.shape[0]
    r_blocks, q_blocks = sub_side // LANES, sub_side // ALIGN
    f_me = lax.axis_index("facet")
    s_me = lax.axis_index("strip")
    me = f_me * n_strip + s_me

    x_loads = []
    for c in range(corr):
        x_low = 0
        for h, (_, _, _, x_high) in enumerate(chunks):
            part = pl.ds(x_low, x_high - x_low)
            x_loads.append(
                [
                    pltpu.make_async_copy(
                        x_ref.at[c, s, part],
                        x_buf.at[c, s, part],
                        load_sem.at[(c * n_chunk + h) * scales + s],
                    )
                    for s in range(scales)
                ]
            )
            x_low = x_high
    others = [
        pltpu.make_async_copy(src, dst, load_sem.at[corr * n_chunk * scales + n])
        for n, (src, dst) in enumerate(
            (
                (index_in, index),
                (offset_in, offsets),
                (frows_in, frows),
                (fcols_in, fcols),
                (observed_in, observed),
            )
        )
    ]
    index_load, offset_load, frows_load, fcols_load, observed_load = others
    col_loads = [
        pltpu.make_async_copy(
            col_in.at[:, pl.ds(b * contrib, contrib)], col_taper.at[b], load_sem.at[corr * n_chunk * scales + 5 + b]
        )
        for b in range(sub_cols)
    ]
    row_loads = [
        pltpu.make_async_copy(
            row_in.at[:, pl.ds(a * contrib, contrib)],
            row_taper.at[a],
            load_sem.at[corr * n_chunk * scales + 5 + sub_cols + a],
        )
        for a in range(sub_rows)
    ]
    for load in x_loads[0]:
        load.start()

    barrier = pltpu.get_barrier_semaphore()
    for off in range(1, n_strip):
        pl.semaphore_signal(
            barrier, inc=1, device_id={"strip": lax.rem(s_me + off, n_strip)}, device_id_type=MESH
        )
    for off in range(1, n_facet):
        pl.semaphore_signal(
            barrier, inc=1, device_id={"facet": lax.rem(f_me + off, n_facet)}, device_id_type=MESH
        )
    fill_bands(taps_ref, pad_ref, across_ref, down_ref, width, chunks)
    y_ref[:, :, 0:LANES] = jnp.zeros((scales, tall, LANES), y_ref.dtype)
    y_ref[:, :, LANES + side : 2 * LANES + side] = jnp.zeros((scales, tall, LANES), y_ref.dtype)
    col_perm = [lax.rem(owner_ref[b], n_strip) for b in range(sub_cols)]
    row_perm = [lax.div(owner_ref[a * sub_cols], n_strip) for a in range(sub_rows)]

    strip_copies = []
    for n_part in range(corr * n_chunk):
        c, h = divmod(n_part, n_chunk)
        low, high, x_low, x_high = chunks[h]
        for s in range(scales):
            x_loads[n_part][s].wait()
            if s == scales - 1 and n_part == 0:
                for load in col_loads + x_loads[1]:
                    load.start()
            if s == scales - 1 and n_part == 1:
                for load in [load for part in x_loads[2:] for load in part] + others + row_loads:
                    load.start()
            for n in range(0, side, COL_TILE):
                y_ref[s, :, LANES + n : LANES + n + COL_TILE] = mm(
                    across_ref[h, s], x_buf[c, s, x_low:x_high, n : n + COL_TILE]
                ).astype(y_ref.dtype)

        def one_tile(tile, carry):
            first = pl.multiple_of(tile * COL_TILE, COL_TILE)
            smoothed = jnp.zeros((tall, COL_TILE), jnp.float32)
            for s in range(scales):
                smoothed += mm(y_ref[s, :, pl.ds(first, COL_TILE + 2 * LANES)], down_ref[s])
            smooth_ref[:, pl.ds(first, COL_TILE)] = smoothed.astype(smooth_ref.dtype)
            return carry

        lax.fori_loop(0, tiles, one_tile, 0, unroll=4)
        if n_part == 0:
            for load in col_loads:
                load.wait()
            pl.semaphore_wait(barrier, n_strip + n_facet - 2)
            for off in range(1, n_strip):
                pl.semaphore_signal(
                    ready_sem,
                    inc=1,
                    device_id={"strip": lax.rem(s_me + off, n_strip)},
                    device_id_type=MESH,
                )
        for first in range(1, n_strip + 1, 2):
            peers = [lax.rem(s_me + off, n_strip) for off in (first, first + 1)]
            pair = jnp.concatenate([col_taper[position_of(col_perm, peer)] for peer in peers], axis=1)
            got = mm(smooth_ref[...], pair).astype(stage.dtype)
            for n, peer in enumerate(peers):
                off = first + n
                part = got[:, n * contrib : (n + 1) * contrib]
                if off == n_strip:
                    grouped[s_me, n_part] = part
                    continue
                stage[n_part, off] = part
                copy = pltpu.make_async_remote_copy(
                    src_ref=stage.at[n_part, off],
                    dst_ref=grouped.at[s_me, n_part],
                    send_sem=strip_send.at[n_part, off],
                    recv_sem=strip_recv.at[n_part, off],
                    device_id={"strip": peer},
                    device_id_type=MESH,
                )
                copy.start()
                strip_copies.append(copy)

    turned[:, r_blocks] = jnp.zeros((corr,) + turned.shape[2:], turned.dtype)
    turned[:, :, q_blocks] = jnp.zeros((corr, r_blocks + 1, ALIGN, LANES), turned.dtype)
    offset_load.wait()
    row_places = lax.broadcasted_iota(jnp.int32, (WIDE, vis), 0)
    col_places = lax.broadcasted_iota(jnp.int32, (TALL, vis), 0)
    factor = -0.5 / (KERNEL_WIDTH * KERNEL_WIDTH)

    def weights(spots, offset):
        delta = spots.astype(jnp.float32) - offset
        inside = (spots >= 0) & (spots < TILE)
        return jnp.where(inside, jnp.exp(factor * (delta * delta)), 0.0)

    def corner(k):
        r, q = corner_ref[0, k], corner_ref[1, k]
        rb = jnp.clip(lax.div(r, LANES), 0, r_blocks - 1)
        qb = jnp.clip(lax.div(q, ALIGN), 0, q_blocks - 2)
        return r - rb * LANES, q - qb * ALIGN, rb, qb

    def one_weight(k, carry):
        r_in, q_in, _, _ = corner(k)
        here = offsets[k]
        row_weights[k] = weights(row_places - r_in, here[0:1]).astype(row_weights.dtype)
        col_weights[k] = weights(col_places - q_in, here[1:2])
        return carry

    lax.fori_loop(0, blocks, one_weight, 0, unroll=2)
    frows_load.wait()
    fcols_load.wait()
    row_mats[...] = jnp.concatenate([frows[f] for f in range(n_facet)], axis=1)
    for load in row_loads:
        load.wait()

    facet_copies = []

    def contribute(c):
        each = n_chunk * (n_strip - 1)
        for copy in strip_copies[c * each : (c + 1) * each]:
            copy.wait()
        head, tail = c * n_chunk, (c + 1) * n_chunk - 1
        flipped = []
        for x in range(n_strip):
            top = grouped[x, head, width : 2 * width]
            bottom = grouped[x, tail, tall - 2 * width : tall - width]
            if x > 0:
                top = plus(top, grouped[x - 1, tail, tall - width : tall])
            if x < n_strip - 1:
                bottom = plus(bottom, grouped[x + 1, head, 0:width])
            middle = []
            for n_part in range(head, tail + 1):
                start = 2 * width if n_part == head else 0
                stop = tall - 2 * width if n_part == tail else tall
                middle.append(grouped[x, n_part, start:stop])
            block = jnp.concatenate([top] + middle + [bottom], axis=0)
            flipped.append(block.T)
        flipped = jnp.concatenate(flipped, axis=1)
        for first in range(n_facet - 1, 0, -2):
            offs = (first, first - 1)
            peers = [flipped_bits(f_me, off, n_facet) for off in offs]
            pair = jnp.concatenate([row_taper[position_of(row_perm, peer)] for peer in peers], axis=1)
            got = mm(flipped, pair).astype(stage2.dtype)
            for n, (off, peer) in enumerate(zip(offs, peers)):
                part = got[:, n * contrib : (n + 1) * contrib]
                if off == 0:
                    mine[f_me, c] = part
                    continue
                stage2[c, off] = part
                copy = pltpu.make_async_remote_copy(
                    src_ref=stage2.at[c, off],
                    dst_ref=mine.at[f_me, c],
                    send_sem=facet_send.at[c, off],
                    recv_sem=facet_recv.at[c, off],
                    device_id={"facet": peer},
                    device_id_type=MESH,
                )
                copy.start()
                facet_copies.append(copy)

    def degrid(c):
        for copy in facet_copies[c * (n_facet - 1) : (c + 1) * (n_facet - 1)]:
            copy.wait()
        for f in range(n_facet):
            spread[c, :, f * contrib : (f + 1) * contrib] = mm(fcols[f], mine[f, c]).astype(spread.dtype)
        for rb in range(r_blocks):
            turned[c, rb, 0:q_blocks] = (
                lax.dot_general(
                    spread[c],
                    row_mats[rb * LANES : (rb + 1) * LANES],
                    ACROSS,
                    preferred_element_type=jnp.float32,
                )
                .astype(turned.dtype)
                .reshape(q_blocks, ALIGN, LANES)
            )

        def one_block(k, carry):
            _, _, rb, qb = corner(k)
            tile = jnp.concatenate(
                [
                    jnp.concatenate([turned[c, rb + j, qb + i] for j in range(2)], axis=1)
                    for i in range(TALL // ALIGN)
                ],
                axis=0,
            )
            along = mm(tile[:, :WIDE], row_weights[k])
            values[pl.ds(c * blocks + k, 1), :] = jnp.sum(along * col_weights[k], axis=0, keepdims=True)
            return carry

        lax.fori_loop(0, blocks, one_block, 0, unroll=8)

    contribute(0)
    index_load.wait()
    for n in range(corr):
        row = gains_ref[n : n + 1, :]
        product[n] = looked_up(row, index[:, 0, :]) * looked_up(row, index[:, 1, :])
    dest = dest_ref[...]
    k_row = lax.broadcasted_iota(jnp.int32, (blocks, blocks), 0)
    k_col = lax.broadcasted_iota(jnp.int32, (blocks, blocks), 1)
    dest_wide = jnp.broadcast_to(dest, (blocks, blocks))
    dest_tall = jnp.sum(jnp.where(k_row == k_col, dest_wide, 0), axis=1, keepdims=True)
    same = (dest_tall == dest_wide) & (k_row < k_col)
    rank = jnp.sum(jnp.where(same, 1, 0), axis=0, keepdims=True)
    target = dest * capacity + rank
    code = jnp.concatenate([target * corr + n for n in range(corr)], axis=1)
    places = lax.broadcasted_iota(jnp.int32, onehot.shape, 0)
    onehot[...] = jnp.where(places == code, 1.0, 0.0).astype(onehot.dtype)
    for c in range(1, corr):
        contribute(c)
        degrid(c - 1)
    degrid(corr - 1)

    outgoing[...] = (
        mm(onehot[...], values[...].astype(jnp.bfloat16))
        .astype(outgoing.dtype)
        .reshape(outgoing.shape)
    )
    pl.semaphore_wait(ready_sem, n_strip - 1)

    vis_copies = []
    for f_off in [n_facet // 2] + [n for n in range(n_facet) if n != n_facet // 2]:
        f_peer = lax.rem(f_me + f_off, n_facet)
        for s_off in range(n_strip):
            if f_off == 0 and s_off == 0:
                continue
            s_peer = lax.rem(s_me + s_off, n_strip)
            off = f_off * n_strip + s_off
            copy = pltpu.make_async_remote_copy(
                src_ref=outgoing.at[f_peer * n_strip + s_peer],
                dst_ref=arrived.at[me],
                send_sem=vis_send.at[off],
                recv_sem=vis_recv.at[off],
                device_id={"facet": f_peer, "strip": s_peer},
                device_id_type=MESH,
            )
            copy.start()
            vis_copies.append(copy)
    arrived[me] = outgoing[me]
    subgrid_copies = []
    for c in range(corr):
        subgrid[c] = lax.dot_general(
            row_mats[...], spread[c], ACROSS, preferred_element_type=jnp.float32
        ).astype(subgrid.dtype)
        copy = pltpu.make_async_copy(subgrid.at[c], subgrid_out.at[c], out_sem.at[c])
        copy.start()
        subgrid_copies.append(copy)
    observed_load.wait()

    for copy in vis_copies:
        copy.wait()
    wide[...] = arrived[...].astype(jnp.float32).reshape(wide.shape)
    for c in range(corr):
        placed = wide[pl.ds(c, devices * capacity, stride=corr), :]
        residual_out[:, c, :] = observed[:, c, :] - product[c] * placed
    for copy in subgrid_copies:
        copy.wait()


def pass_kernel(a_ref, b_ref, a_out, b_out, a_buf, b_buf, in_sem, out_sem):
    parts = a_ref.shape[0]
    pairs = [(a_ref.at[n], a_buf.at[n], a_out.at[n]) for n in range(parts)]
    pairs.append((b_ref, b_buf, b_out))
    loads = [pltpu.make_async_copy(src, buf, in_sem.at[n]) for n, (src, buf, _) in enumerate(pairs)]
    stores = [pltpu.make_async_copy(buf, dst, out_sem.at[n]) for n, (_, buf, dst) in enumerate(pairs)]
    for load in loads:
        load.start()
    for load, store in zip(loads, stores):
        load.wait()
        store.start()
    for store in stores:
        store.wait()


def handed_on(subgrid, residual):
    parts = 8
    cut = subgrid.reshape(parts, -1, subgrid.shape[-1])
    remote = pl.BlockSpec(memory_space=pl.ANY)
    a, b = pl.pallas_call(
        pass_kernel,
        in_specs=[remote, remote],
        out_specs=[remote, remote],
        out_shape=[
            jax.ShapeDtypeStruct(cut.shape, cut.dtype),
            jax.ShapeDtypeStruct(residual.shape, residual.dtype),
        ],
        scratch_shapes=[
            pltpu.VMEM(cut.shape, cut.dtype),
            pltpu.VMEM(residual.shape, residual.dtype),
            pltpu.SemaphoreType.DMA((parts + 1,)),
            pltpu.SemaphoreType.DMA((parts + 1,)),
        ],
        name="handed_on",
    )(cut, residual)
    return a.reshape(subgrid.shape), b


def on_device(
    sky_components,
    scale_kernels,
    row_taper,
    col_taper,
    finish_rows,
    finish_cols,
    subgrid_owner,
    block_cell,
    vis_offset,
    block_owner,
    observed,
    antenna_pair_index,
    gains,
):
    n_facet = lax.axis_size("facet")
    n_strip = lax.axis_size("strip")
    devices = n_facet * n_strip
    comp = sky_components[0]
    corr, scales, rows, side = comp.shape
    chunks = row_chunks(rows, (scale_kernels.shape[1] - 1) // 2)
    n_chunk = len(chunks)
    tall = chunks[0][1] - chunks[0][0]
    sub_side, contrib = finish_cols.shape[1], finish_cols.shape[2]
    blocks, _, vis = vis_offset.shape
    sub_rows, sub_cols = row_taper.shape[2] // contrib, col_taper.shape[2] // contrib
    slots = observed.shape[0]
    per_device = slots // devices * corr
    whole = pl.BlockSpec(memory_space=pltpu.VMEM)
    scalars = pl.BlockSpec(memory_space=pltpu.SMEM)
    remote = pl.BlockSpec(memory_space=pl.ANY)
    bf16, f32 = jnp.bfloat16, jnp.float32
    dma = pltpu.SemaphoreType.DMA
    subgrid, residual = pl.pallas_call(
        functools.partial(whole_kernel, n_facet, n_strip),
        in_specs=[scalars, scalars, whole, whole, whole] + [remote] * 8,
        out_specs=[remote, whole],
        out_shape=[
            jax.ShapeDtypeStruct((corr, sub_side, sub_side), bf16),
            jax.ShapeDtypeStruct(observed.shape, f32),
        ],
        scratch_shapes=[
            pltpu.VMEM((corr, scales, rows, side), bf16),
            pltpu.VMEM((sub_cols, side, contrib), bf16),
            pltpu.VMEM((sub_rows, side, contrib), bf16),
            pltpu.VMEM(finish_rows.shape, bf16),
            pltpu.VMEM(finish_cols.shape, bf16),
            pltpu.VMEM(vis_offset.shape, f32),
            pltpu.VMEM(antenna_pair_index.shape, jnp.int32),
            pltpu.VMEM(observed.shape, f32),
            pltpu.VMEM((scales, 2 * LANES), f32),
            pltpu.VMEM((n_chunk, scales, tall, chunks[0][3] - chunks[0][2]), bf16),
            pltpu.VMEM((scales, COL_TILE + 2 * LANES, COL_TILE), bf16),
            pltpu.VMEM((scales, tall, side + 2 * LANES), bf16),
            pltpu.VMEM((tall, side), bf16),
            pltpu.VMEM((corr * n_chunk, n_strip, tall, contrib), bf16),
            pltpu.VMEM((n_strip, corr * n_chunk, tall, contrib), bf16),
            pltpu.VMEM((corr, n_facet, contrib, contrib), bf16),
            pltpu.VMEM((n_facet, corr, contrib, contrib), bf16),
            pltpu.VMEM((sub_side, n_facet * contrib), bf16),
            pltpu.VMEM((corr, sub_side, n_facet * contrib), bf16),
            pltpu.VMEM((corr, sub_side // LANES + 1, sub_side // ALIGN + 1, ALIGN, LANES), bf16),
            pltpu.VMEM((corr, sub_side, sub_side), bf16),
            pltpu.VMEM((blocks, WIDE, vis), bf16),
            pltpu.VMEM((blocks, TALL, vis), f32),
            pltpu.VMEM((devices * per_device, corr * blocks), bf16),
            pltpu.VMEM((corr * blocks, vis), f32),
            pltpu.VMEM((devices, per_device, vis), bf16),
            pltpu.VMEM((devices, per_device, vis), bf16),
            pltpu.VMEM((devices * per_device, vis), f32),
            pltpu.VMEM((corr, slots, vis), f32),
            dma((corr * n_chunk * scales + 5 + sub_cols + sub_rows,)),
            dma((corr * n_chunk, n_strip)),
            dma((corr * n_chunk, n_strip)),
            dma((corr, n_facet)),
            dma((corr, n_facet)),
            dma((devices,)),
            dma((devices,)),
            dma((corr,)),
            pltpu.SemaphoreType.REGULAR,
        ],
        compiler_params=pltpu.CompilerParams(
            collective_id=0, has_side_effects=True, vmem_limit_bytes=60 * 1024 * 1024
        ),
        name="sky_to_residual",
    )(
        subgrid_owner,
        block_cell.T,
        scale_kernels,
        block_owner.reshape(1, blocks),
        gains,
        comp,
        col_taper[0],
        row_taper[0],
        finish_rows,
        finish_cols,
        vis_offset,
        antenna_pair_index,
        observed,
    )
    subgrid, residual = handed_on(subgrid, residual)
    return subgrid[None], residual


def solution(mesh):
    placed = (
        P("facet", None, None, "strip", None),
        P(),
        P("facet", None, None),
        P("facet", None, None),
        P(),
        P(),
        P(),
        P(("facet", "strip"), None),
        P(("facet", "strip"), None, None),
        P(("facet", "strip"), None),
        P(("facet", "strip"), None, None),
        P(("facet", "strip"), None, None),
        P(),
    )
    return jax.shard_map(
        on_device,
        mesh=mesh,
        in_specs=placed,
        out_specs=(P(("facet", "strip"), None, None, None), P(("facet", "strip"), None, None)),
        check_vma=False,
    )
```

```python
import functools

import jax
import jax.numpy as jnp
from jax import lax
from jax.experimental import pallas as pl
from jax.experimental.pallas import tpu as pltpu
from jax.sharding import PartitionSpec as P

TILE = 32
KERNEL_WIDTH = 1.5
LANES = 128
COL_TILE = 256
ALIGN = 16
TALL = TILE + ALIGN
WIDE = LANES + TILE
MESH = pl.DeviceIdType.MESH
ACROSS = (((1,), (1,)), ((), ()))


def mm(a, b):
    return jnp.dot(a, b, preferred_element_type=jnp.float32)


def row_chunks(rows, width):
    count = rows // LANES
    chunks = []
    for h in range(count):
        low = h * LANES if h else -width
        high = (h + 1) * LANES if h < count - 1 else rows + width
        chunks.append((low, high, max(0, low - width), min(rows, high + width)))
    return chunks


def fill_bands(taps_ref, pad_ref, across_ref, down_ref, width, chunks):
    scales, taps = taps_ref.shape
    span = LANES + taps - 1
    pad_ref[...] = jnp.zeros_like(pad_ref)
    pad_ref[:, 0:taps] = taps_ref[...]
    down_ref[...] = jnp.zeros_like(down_ref)
    for s in range(scales):
        row = jnp.broadcast_to(pad_ref[s : s + 1, :], (LANES, 2 * LANES))
        band = pltpu.roll(row, 0, 1, stride=1, stride_axis=0)
        down = band.T[:span].astype(down_ref.dtype)
        for tile in range(COL_TILE // LANES):
            start = LANES - width + tile * LANES
            down_ref[s, start : start + span, tile * LANES : (tile + 1) * LANES] = down
        for h, (low, high, x_low, x_high) in enumerate(chunks):
            for first in range(0, high - low, LANES):
                size = min(LANES, high - low - first)
                line = jnp.broadcast_to(pad_ref[s : s + 1, :], (size, 2 * LANES))
                shift = (low - width - x_low + first) % (2 * LANES)
                if shift:
                    line = pltpu.roll(line, shift, 1)
                line = pltpu.roll(line, 0, 1, stride=1, stride_axis=0)
                across_ref[h, s, first : first + size] = line[:, 0 : x_high - x_low].astype(
                    across_ref.dtype
                )


def plus(a, b):
    return (a.astype(jnp.float32) + b.astype(jnp.float32)).astype(a.dtype)


def position_of(values, wanted):
    place = 0
    for j, value in enumerate(values):
        gap = value - wanted
        place += j * jnp.maximum(1 - gap * gap, 0)
    return jnp.minimum(place, len(values) - 1)


def looked_up(row, index):
    low, high = index % LANES, index // LANES
    out = None
    for chunk in range(row.shape[1] // LANES):
        table = jnp.broadcast_to(row[:, chunk * LANES : (chunk + 1) * LANES], index.shape)
        got = jnp.take_along_axis(table, low, axis=1, mode="promise_in_bounds")
        out = got if out is None else jnp.where(high == chunk, got, out)
    return out


def whole_kernel(
    n_facet,
    n_strip,
    owner_ref,
    corner_ref,
    taps_ref,
    dest_ref,
    gains_ref,
    x_ref,
    col_in,
    row_in,
    frows_in,
    fcols_in,
    offset_in,
    index_in,
    subgrid_out,
    arrived,
    product_out,
    x_buf,
    col_taper,
    row_taper,
    frows,
    fcols,
    offsets,
    index,
    pad_ref,
    across_ref,
    down_ref,
    y_ref,
    smooth_ref,
    stage,
    grouped,
    stage2,
    mine,
    row_mats,
    spread,
    turned,
    subgrid,
    row_weights,
    col_weights,
    onehot,
    values,
    outgoing,
    product,
    load_sem,
    strip_send,
    strip_recv,
    facet_send,
    facet_recv,
    vis_send,
    vis_recv,
    out_sem,
    ready_sem,
    wave_sem,
):
    corr, scales, rows, side = x_ref.shape
    width = (taps_ref.shape[1] - 1) // 2
    chunks = row_chunks(rows, width)
    n_chunk = len(chunks)
    tall = chunks[0][1] - chunks[0][0]
    tiles = side // COL_TILE
    contrib = fcols.shape[2]
    sub_side = fcols.shape[1]
    blocks = offsets.shape[0]
    vis = offsets.shape[2]
    devices = n_facet * n_strip
    capacity = outgoing.shape[1] // corr
    sub_cols = col_taper.shape[0]
    sub_rows = row_taper.shape[0]
    r_blocks, q_blocks = sub_side // LANES, sub_side // ALIGN
    f_me = lax.axis_index("facet")
    s_me = lax.axis_index("strip")
    me = f_me * n_strip + s_me

    x_loads = []
    for c in range(corr):
        x_low = 0
        for h, (_, _, _, x_high) in enumerate(chunks):
            part = pl.ds(x_low, x_high - x_low)
            x_loads.append(
                pltpu.make_async_copy(
                    x_ref.at[c, :, part], x_buf.at[c, :, part], load_sem.at[c * n_chunk + h]
                )
            )
            x_low = x_high
    others = [
        pltpu.make_async_copy(src, dst, load_sem.at[corr * n_chunk + n])
        for n, (src, dst) in enumerate(
            (
                (index_in, index),
                (offset_in, offsets),
                (frows_in, frows),
                (fcols_in, fcols),
            )
        )
    ]
    index_load, offset_load, frows_load, fcols_load = others
    col_loads = [
        pltpu.make_async_copy(
            col_in.at[:, pl.ds(b * contrib, contrib)], col_taper.at[b], load_sem.at[corr * n_chunk + 4 + b]
        )
        for b in range(sub_cols)
    ]
    row_loads = [
        pltpu.make_async_copy(
            row_in.at[:, pl.ds(a * contrib, contrib)],
            row_taper.at[a],
            load_sem.at[corr * n_chunk + 4 + sub_cols + a],
        )
        for a in range(sub_rows)
    ]
    for load in x_loads[:n_chunk] + col_loads + x_loads[n_chunk:] + others + row_loads:
        load.start()

    barrier = pltpu.get_barrier_semaphore()
    for off in range(1, n_strip):
        pl.semaphore_signal(
            barrier, inc=1, device_id={"strip": lax.rem(s_me + off, n_strip)}, device_id_type=MESH
        )
    near = jnp.minimum(f_me, 1) + jnp.minimum(n_facet - 1 - f_me, 1)

    def signal_near(sem):
        @pl.when(f_me > 0)
        def _():
            pl.semaphore_signal(sem, inc=1, device_id={"facet": f_me - 1}, device_id_type=MESH)

        @pl.when(f_me < n_facet - 1)
        def _():
            pl.semaphore_signal(sem, inc=1, device_id={"facet": f_me + 1}, device_id_type=MESH)

    signal_near(barrier)
    fill_bands(taps_ref, pad_ref, across_ref, down_ref, width, chunks)
    y_ref[:, :, 0:LANES] = jnp.zeros((scales, tall, LANES), y_ref.dtype)
    y_ref[:, :, LANES + side : 2 * LANES + side] = jnp.zeros((scales, tall, LANES), y_ref.dtype)
    col_perm = [lax.rem(owner_ref[b], n_strip) for b in range(sub_cols)]
    row_perm = [lax.div(owner_ref[a * sub_cols], n_strip) for a in range(sub_rows)]

    strip_copies = []
    for n_part in range(corr * n_chunk):
        c, h = divmod(n_part, n_chunk)
        low, high, x_low, x_high = chunks[h]
        x_loads[n_part].wait()
        for s in range(scales):
            for n in range(0, side, COL_TILE):
                y_ref[s, :, LANES + n : LANES + n + COL_TILE] = mm(
                    across_ref[h, s], x_buf[c, s, x_low:x_high, n : n + COL_TILE]
                ).astype(y_ref.dtype)

        def one_tile(tile, carry):
            first = pl.multiple_of(tile * COL_TILE, COL_TILE)
            smoothed = jnp.zeros((tall, COL_TILE), jnp.float32)
            for s in range(scales):
                smoothed += mm(y_ref[s, :, pl.ds(first, COL_TILE + 2 * LANES)], down_ref[s])
            smooth_ref[:, pl.ds(first, COL_TILE)] = smoothed.astype(smooth_ref.dtype)
            return carry

        lax.fori_loop(0, tiles, one_tile, 0, unroll=4)
        if n_part == 0:
            for load in col_loads:
                load.wait()
            pl.semaphore_wait(barrier, n_strip - 1 + near)
            signal_near(wave_sem.at[0])
        for first in range(1, n_strip + 1, 2):
            peers = [lax.rem(s_me + off, n_strip) for off in (first, first + 1)]
            pair = jnp.concatenate([col_taper[position_of(col_perm, peer)] for peer in peers], axis=1)
            got = mm(smooth_ref[...], pair).astype(stage.dtype)
            for n, peer in enumerate(peers):
                off = first + n
                part = got[:, n * contrib : (n + 1) * contrib]
                if off == n_strip:
                    grouped[s_me, n_part] = part
                    continue
                stage[n_part, off] = part
                copy = pltpu.make_async_remote_copy(
                    src_ref=stage.at[n_part, off],
                    dst_ref=grouped.at[s_me, n_part],
                    send_sem=strip_send.at[n_part, off],
                    recv_sem=strip_recv.at[n_part, off],
                    device_id={"strip": peer},
                    device_id_type=MESH,
                )
                copy.start()
                strip_copies.append(copy)
        if n_part == 0:
            continue
        last = n_part == corr * n_chunk - 1
        for wave in range(n_part - 1, n_facet - 2 if last else n_part):
            if wave < n_facet - 2:
                pl.semaphore_wait(wave_sem.at[wave], near)
            if wave + 1 < n_facet - 2:
                signal_near(wave_sem.at[wave + 1])
    for off in range(1, n_strip):
        pl.semaphore_signal(
            ready_sem, inc=1, device_id={"strip": lax.rem(s_me + off, n_strip)}, device_id_type=MESH
        )

    turned[:, r_blocks] = jnp.zeros((corr,) + turned.shape[2:], turned.dtype)
    turned[:, :, q_blocks] = jnp.zeros((corr, r_blocks + 1, ALIGN, LANES), turned.dtype)
    offset_load.wait()
    row_places = lax.broadcasted_iota(jnp.int32, (WIDE, vis), 0)
    col_places = lax.broadcasted_iota(jnp.int32, (TALL, vis), 0)
    factor = -0.5 / (KERNEL_WIDTH * KERNEL_WIDTH)

    def weights(spots, offset):
        delta = spots.astype(jnp.float32) - offset
        inside = (spots >= 0) & (spots < TILE)
        return jnp.where(inside, jnp.exp(factor * (delta * delta)), 0.0)

    def corner(k):
        r, q = corner_ref[0, k], corner_ref[1, k]
        rb = jnp.clip(lax.div(r, LANES), 0, r_blocks - 1)
        qb = jnp.clip(lax.div(q, ALIGN), 0, q_blocks - 2)
        return r - rb * LANES, q - qb * ALIGN, rb, qb

    def one_weight(k, carry):
        r_in, q_in, _, _ = corner(k)
        here = offsets[k]
        row_weights[k] = weights(row_places - r_in, here[0:1]).astype(row_weights.dtype)
        col_weights[k] = weights(col_places - q_in, here[1:2])
        return carry

    lax.fori_loop(0, blocks, one_weight, 0, unroll=2)
    frows_load.wait()
    fcols_load.wait()
    row_mats[...] = jnp.concatenate([frows[f] for f in range(n_facet)], axis=1)
    for load in row_loads:
        load.wait()

    facet_copies = []

    def contribute(c):
        each = n_chunk * (n_strip - 1)
        for copy in strip_copies[c * each : (c + 1) * each]:
            copy.wait()
        head, tail = c * n_chunk, (c + 1) * n_chunk - 1
        flipped = []
        for x in range(n_strip):
            top = grouped[x, head, width : 2 * width]
            bottom = grouped[x, tail, tall - 2 * width : tall - width]
            if x > 0:
                top = plus(top, grouped[x - 1, tail, tall - width : tall])
            if x < n_strip - 1:
                bottom = plus(bottom, grouped[x + 1, head, 0:width])
            middle = []
            for n_part in range(head, tail + 1):
                start = 2 * width if n_part == head else 0
                stop = tall - 2 * width if n_part == tail else tall
                middle.append(grouped[x, n_part, start:stop])
            block = jnp.concatenate([top] + middle + [bottom], axis=0)
            flipped.append(block.T)
        flipped = jnp.concatenate(flipped, axis=1)
        for first in range(1, n_facet + 1, 2):
            peers = [lax.rem(f_me + off, n_facet) for off in (first, first + 1)]
            pair = jnp.concatenate([row_taper[position_of(row_perm, peer)] for peer in peers], axis=1)
            got = mm(flipped, pair).astype(stage2.dtype)
            for n, peer in enumerate(peers):
                off = first + n
                part = got[:, n * contrib : (n + 1) * contrib]
                if off == n_facet:
                    mine[f_me, c] = part
                    continue
                stage2[c, off] = part
                copy = pltpu.make_async_remote_copy(
                    src_ref=stage2.at[c, off],
                    dst_ref=mine.at[f_me, c],
                    send_sem=facet_send.at[c, off],
                    recv_sem=facet_recv.at[c, off],
                    device_id={"facet": peer},
                    device_id_type=MESH,
                )
                copy.start()
                facet_copies.append(copy)

    def degrid(c):
        for copy in facet_copies[c * (n_facet - 1) : (c + 1) * (n_facet - 1)]:
            copy.wait()
        for f in range(n_facet):
            spread[c, :, f * contrib : (f + 1) * contrib] = mm(fcols[f], mine[f, c]).astype(spread.dtype)
        for rb in range(r_blocks):
            turned[c, rb, 0:q_blocks] = (
                lax.dot_general(
                    spread[c],
                    row_mats[rb * LANES : (rb + 1) * LANES],
                    ACROSS,
                    preferred_element_type=jnp.float32,
                )
                .astype(turned.dtype)
                .reshape(q_blocks, ALIGN, LANES)
            )

        def one_block(k, carry):
            _, _, rb, qb = corner(k)
            tile = jnp.concatenate(
                [
                    jnp.concatenate([turned[c, rb + j, qb + i] for j in range(2)], axis=1)
                    for i in range(TALL // ALIGN)
                ],
                axis=0,
            )
            along = mm(tile[:, :WIDE], row_weights[k])
            values[pl.ds(c * blocks + k, 1), :] = jnp.sum(along * col_weights[k], axis=0, keepdims=True)
            return carry

        lax.fori_loop(0, blocks, one_block, 0, unroll=16)

    contribute(0)
    index_load.wait()
    for n in range(corr):
        row = gains_ref[n : n + 1, :]
        product[n] = looked_up(row, index[:, 0, :]) * looked_up(row, index[:, 1, :])
    product_copy = pltpu.make_async_copy(product, product_out, out_sem.at[corr])
    product_copy.start()
    dest = dest_ref[...]
    k_row = lax.broadcasted_iota(jnp.int32, (blocks, blocks), 0)
    k_col = lax.broadcasted_iota(jnp.int32, (blocks, blocks), 1)
    dest_wide = jnp.broadcast_to(dest, (blocks, blocks))
    dest_tall = jnp.sum(jnp.where(k_row == k_col, dest_wide, 0), axis=1, keepdims=True)
    same = (dest_tall == dest_wide) & (k_row < k_col)
    rank = jnp.sum(jnp.where(same, 1, 0), axis=0, keepdims=True)
    target = dest * capacity + rank
    code = jnp.concatenate([target * corr + n for n in range(corr)], axis=1)
    places = lax.broadcasted_iota(jnp.int32, onehot.shape, 0)
    onehot[...] = jnp.where(places == code, 1.0, 0.0).astype(onehot.dtype)
    for c in range(1, corr):
        contribute(c)
        degrid(c - 1)
    degrid(corr - 1)

    outgoing[...] = (
        mm(onehot[...], values[...].astype(jnp.bfloat16))
        .astype(outgoing.dtype)
        .reshape(outgoing.shape)
    )
    pl.semaphore_wait(ready_sem, n_strip - 1)

    vis_copies = []
    for f_off in [n_facet // 2] + [n for n in range(n_facet) if n != n_facet // 2]:
        f_peer = lax.rem(f_me + f_off, n_facet)
        for s_off in range(n_strip):
            if f_off == 0 and s_off == 0:
                continue
            s_peer = lax.rem(s_me + s_off, n_strip)
            off = f_off * n_strip + s_off
            copy = pltpu.make_async_remote_copy(
                src_ref=outgoing.at[f_peer * n_strip + s_peer],
                dst_ref=arrived.at[me],
                send_sem=vis_send.at[off],
                recv_sem=vis_recv.at[off],
                device_id={"facet": f_peer, "strip": s_peer},
                device_id_type=MESH,
            )
            copy.start()
            vis_copies.append(copy)
    own_copy = pltpu.make_async_copy(outgoing.at[me], arrived.at[me], out_sem.at[corr + 1])
    own_copy.start()
    subgrid_copies = [product_copy, own_copy]
    for c in range(corr):
        subgrid[c] = lax.dot_general(
            row_mats[...], spread[c], ACROSS, preferred_element_type=jnp.float32
        ).astype(subgrid.dtype)
        copy = pltpu.make_async_copy(subgrid.at[c], subgrid_out.at[c], out_sem.at[c])
        copy.start()
        subgrid_copies.append(copy)

    for copy in vis_copies:
        copy.wait()
    for copy in subgrid_copies:
        copy.wait()


def close_kernel(
    subgrid_in, arrived_in, product_in, observed_in, subgrid_out, residual_out,
    subgrid, arrived, product, observed, residual, wide, in_sem, out_sem,
):
    parts = subgrid_in.shape[0]
    corr, slots = product.shape[:2]
    small = ((arrived_in, arrived), (product_in, product), (observed_in, observed))
    loads = [
        pltpu.make_async_copy(src, dst, in_sem.at[parts + n]) for n, (src, dst) in enumerate(small)
    ]
    cut_loads = [
        pltpu.make_async_copy(subgrid_in.at[n], subgrid.at[n], in_sem.at[n]) for n in range(parts)
    ]
    stores = [
        pltpu.make_async_copy(subgrid.at[n], subgrid_out.at[n], out_sem.at[n]) for n in range(parts)
    ]
    for load in loads + cut_loads:
        load.start()
    for load in loads:
        load.wait()
    wide[...] = arrived[...].astype(jnp.float32).reshape(wide.shape)
    for c in range(corr):
        placed = wide[pl.ds(c, slots, stride=corr), :]
        residual[:, c, :] = observed[:, c, :] - product[c] * placed
    stores.append(pltpu.make_async_copy(residual, residual_out, out_sem.at[parts]))
    stores[-1].start()
    for load, store in zip(cut_loads, stores):
        load.wait()
        store.start()
    for store in stores:
        store.wait()


def closed(subgrid, arrived, product, observed):
    parts = 4
    cut = subgrid.reshape(parts, -1, subgrid.shape[-1])
    remote = pl.BlockSpec(memory_space=pl.ANY)
    a, b = pl.pallas_call(
        close_kernel,
        in_specs=[remote] * 4,
        out_specs=[remote, remote],
        out_shape=[
            jax.ShapeDtypeStruct(cut.shape, cut.dtype),
            jax.ShapeDtypeStruct(observed.shape, observed.dtype),
        ],
        scratch_shapes=[
            pltpu.VMEM(cut.shape, cut.dtype),
            pltpu.VMEM(arrived.shape, arrived.dtype),
            pltpu.VMEM(product.shape, product.dtype),
            pltpu.VMEM(observed.shape, observed.dtype),
            pltpu.VMEM(observed.shape, observed.dtype),
            pltpu.VMEM((arrived.shape[0] * arrived.shape[1], arrived.shape[2]), jnp.float32),
            pltpu.SemaphoreType.DMA((parts + 3,)),
            pltpu.SemaphoreType.DMA((parts + 1,)),
        ],
        name="closed",
    )(cut, arrived, product, observed)
    return a.reshape(subgrid.shape), b


def on_device(
    sky_components,
    scale_kernels,
    row_taper,
    col_taper,
    finish_rows,
    finish_cols,
    subgrid_owner,
    block_cell,
    vis_offset,
    block_owner,
    observed,
    antenna_pair_index,
    gains,
):
    n_facet = lax.axis_size("facet")
    n_strip = lax.axis_size("strip")
    devices = n_facet * n_strip
    comp = sky_components[0]
    corr, scales, rows, side = comp.shape
    chunks = row_chunks(rows, (scale_kernels.shape[1] - 1) // 2)
    n_chunk = len(chunks)
    tall = chunks[0][1] - chunks[0][0]
    sub_side, contrib = finish_cols.shape[1], finish_cols.shape[2]
    blocks, _, vis = vis_offset.shape
    sub_rows, sub_cols = row_taper.shape[2] // contrib, col_taper.shape[2] // contrib
    slots = observed.shape[0]
    per_device = slots // devices * corr
    whole = pl.BlockSpec(memory_space=pltpu.VMEM)
    scalars = pl.BlockSpec(memory_space=pltpu.SMEM)
    remote = pl.BlockSpec(memory_space=pl.ANY)
    bf16, f32 = jnp.bfloat16, jnp.float32
    dma = pltpu.SemaphoreType.DMA
    subgrid, arrived, product = pl.pallas_call(
        functools.partial(whole_kernel, n_facet, n_strip),
        in_specs=[scalars, scalars, whole, whole, whole] + [remote] * 7,
        out_specs=[remote] * 3,
        out_shape=[
            jax.ShapeDtypeStruct((corr, sub_side, sub_side), bf16),
            jax.ShapeDtypeStruct((devices, per_device, vis), bf16),
            jax.ShapeDtypeStruct((corr, slots, vis), f32),
        ],
        scratch_shapes=[
            pltpu.VMEM((corr, scales, rows, side), bf16),
            pltpu.VMEM((sub_cols, side, contrib), bf16),
            pltpu.VMEM((sub_rows, side, contrib), bf16),
            pltpu.VMEM(finish_rows.shape, bf16),
            pltpu.VMEM(finish_cols.shape, bf16),
            pltpu.VMEM(vis_offset.shape, f32),
            pltpu.VMEM(antenna_pair_index.shape, jnp.int32),
            pltpu.VMEM((scales, 2 * LANES), f32),
            pltpu.VMEM((n_chunk, scales, tall, chunks[0][3] - chunks[0][2]), bf16),
            pltpu.VMEM((scales, COL_TILE + 2 * LANES, COL_TILE), bf16),
            pltpu.VMEM((scales, tall, side + 2 * LANES), bf16),
            pltpu.VMEM((tall, side), bf16),
            pltpu.VMEM((corr * n_chunk, n_strip, tall, contrib), bf16),
            pltpu.VMEM((n_strip, corr * n_chunk, tall, contrib), bf16),
            pltpu.VMEM((corr, n_facet, contrib, contrib), bf16),
            pltpu.VMEM((n_facet, corr, contrib, contrib), bf16),
            pltpu.VMEM((sub_side, n_facet * contrib), bf16),
            pltpu.VMEM((corr, sub_side, n_facet * contrib), bf16),
            pltpu.VMEM((corr, sub_side // LANES + 1, sub_side // ALIGN + 1, ALIGN, LANES), bf16),
            pltpu.VMEM((corr, sub_side, sub_side), bf16),
            pltpu.VMEM((blocks, WIDE, vis), bf16),
            pltpu.VMEM((blocks, TALL, vis), f32),
            pltpu.VMEM((devices * per_device, corr * blocks), bf16),
            pltpu.VMEM((corr * blocks, vis), f32),
            pltpu.VMEM((devices, per_device, vis), bf16),
            pltpu.VMEM((corr, slots, vis), f32),
            dma((corr * n_chunk + 4 + sub_cols + sub_rows,)),
            dma((corr * n_chunk, n_strip)),
            dma((corr * n_chunk, n_strip)),
            dma((corr, n_facet)),
            dma((corr, n_facet)),
            dma((devices,)),
            dma((devices,)),
            dma((corr + 2,)),
            pltpu.SemaphoreType.REGULAR,
            pltpu.SemaphoreType.REGULAR((max(n_facet - 2, 1),)),
        ],
        compiler_params=pltpu.CompilerParams(
            collective_id=0, has_side_effects=True, vmem_limit_bytes=60 * 1024 * 1024
        ),
        name="sky_to_residual",
    )(
        subgrid_owner,
        block_cell.T,
        scale_kernels,
        block_owner.reshape(1, blocks),
        gains,
        comp,
        col_taper[0],
        row_taper[0],
        finish_rows,
        finish_cols,
        vis_offset,
        antenna_pair_index,
    )
    subgrid, residual = closed(subgrid, arrived, product, observed)
    return subgrid[None], residual


def solution(mesh):
    placed = (
        P("facet", None, None, "strip", None),
        P(),
        P("facet", None, None),
        P("facet", None, None),
        P(),
        P(),
        P(),
        P(("facet", "strip"), None),
        P(("facet", "strip"), None, None),
        P(("facet", "strip"), None),
        P(("facet", "strip"), None, None),
        P(("facet", "strip"), None, None),
        P(),
    )
    return jax.shard_map(
        on_device,
        mesh=mesh,
        in_specs=placed,
        out_specs=(P(("facet", "strip"), None, None, None), P(("facet", "strip"), None, None)),
        check_vma=False,
    )
```

```python
import functools

import jax
import jax.numpy as jnp
from jax import lax
from jax.experimental import pallas as pl
from jax.experimental.pallas import tpu as pltpu
from jax.sharding import PartitionSpec as P

TILE = 32
KERNEL_WIDTH = 1.5
LANES = 128
COL_TILE = 256
BAND = COL_TILE + LANES
ALIGN = 16
TALL = TILE + ALIGN
WIDE = LANES + TILE
MESH = pl.DeviceIdType.MESH
ACROSS = (((1,), (1,)), ((), ()))


def mm(a, b):
    return jnp.dot(a, b, preferred_element_type=jnp.float32)


def row_chunks(rows, width):
    count = max(1, rows // COL_TILE)
    step = rows // count
    chunks = []
    for h in range(count):
        low = h * step if h else -width
        high = (h + 1) * step if h < count - 1 else rows + width
        chunks.append((low, high, max(0, low - width), min(rows, high + width)))
    return chunks


def fill_bands(taps_ref, pad_ref, across_ref, down_ref, width, chunks):
    scales, taps = taps_ref.shape
    span = LANES + taps - 1
    pad_ref[...] = jnp.zeros_like(pad_ref)
    pad_ref[:, 0:taps] = taps_ref[...]
    down_ref[...] = jnp.zeros_like(down_ref)
    for s in range(scales):
        row = jnp.broadcast_to(pad_ref[s : s + 1, 0 : 2 * LANES], (LANES, 2 * LANES))
        band = pltpu.roll(row, 0, 1, stride=1, stride_axis=0)
        down = band.T[:span].astype(down_ref.dtype)
        for tile in range(COL_TILE // LANES):
            start = LANES - width + tile * LANES
            down_ref[s, start : start + span, tile * LANES : (tile + 1) * LANES] = down
        for h, (low, high, x_low, x_high) in enumerate(chunks):
            for first in range(0, high - low, LANES):
                size = min(LANES, high - low - first)
                line = jnp.broadcast_to(pad_ref[s : s + 1, :], (size, BAND))
                shift = (low - width - x_low + first) % BAND
                if shift:
                    line = pltpu.roll(line, shift, 1)
                line = pltpu.roll(line, 0, 1, stride=1, stride_axis=0)
                across_ref[h, s, first : first + size] = line[:, 0 : x_high - x_low].astype(
                    across_ref.dtype
                )


def plus(a, b):
    return (a.astype(jnp.float32) + b.astype(jnp.float32)).astype(a.dtype)


def position_of(values, wanted):
    place = 0
    for j, value in enumerate(values):
        gap = value - wanted
        place += j * jnp.maximum(1 - gap * gap, 0)
    return jnp.minimum(place, len(values) - 1)


def looked_up(row, index):
    low, high = index % LANES, index // LANES
    out = None
    for chunk in range(row.shape[1] // LANES):
        table = jnp.broadcast_to(row[:, chunk * LANES : (chunk + 1) * LANES], index.shape)
        got = jnp.take_along_axis(table, low, axis=1, mode="promise_in_bounds")
        out = got if out is None else jnp.where(high == chunk, got, out)
    return out


def whole_kernel(
    n_facet,
    n_strip,
    owner_ref,
    corner_ref,
    taps_ref,
    dest_ref,
    gains_ref,
    x_ref,
    col_in,
    row_in,
    frows_in,
    fcols_in,
    offset_in,
    index_in,
    subgrid_out,
    arrived,
    product_out,
    x_buf,
    col_taper,
    row_taper,
    frows,
    fcols,
    offsets,
    index,
    pad_ref,
    across_ref,
    down_ref,
    y_ref,
    smooth_ref,
    stage,
    grouped,
    stage2,
    mine,
    row_mats,
    spread,
    turned,
    subgrid,
    row_weights,
    col_weights,
    onehot,
    values,
    outgoing,
    product,
    load_sem,
    strip_send,
    strip_recv,
    facet_send,
    facet_recv,
    vis_send,
    vis_recv,
    out_sem,
    ready_sem,
    wave_sem,
):
    corr, scales, rows, side = x_ref.shape
    width = (taps_ref.shape[1] - 1) // 2
    chunks = row_chunks(rows, width)
    n_chunk = len(chunks)
    tall = chunks[0][1] - chunks[0][0]
    tiles = side // COL_TILE
    contrib = fcols.shape[2]
    sub_side = fcols.shape[1]
    blocks = offsets.shape[0]
    vis = offsets.shape[2]
    devices = n_facet * n_strip
    capacity = outgoing.shape[1] // corr
    sub_cols = col_taper.shape[0]
    sub_rows = row_taper.shape[0]
    r_blocks, q_blocks = sub_side // LANES, sub_side // ALIGN
    f_me = lax.axis_index("facet")
    s_me = lax.axis_index("strip")
    me = f_me * n_strip + s_me

    x_loads = []
    for c in range(corr):
        x_low = 0
        for h, (_, _, _, x_high) in enumerate(chunks):
            part = pl.ds(x_low, x_high - x_low)
            x_loads.append(
                pltpu.make_async_copy(
                    x_ref.at[c, :, part], x_buf.at[c, :, part], load_sem.at[c * n_chunk + h]
                )
            )
            x_low = x_high
    others = [
        pltpu.make_async_copy(src, dst, load_sem.at[corr * n_chunk + n])
        for n, (src, dst) in enumerate(
            (
                (index_in, index),
                (offset_in, offsets),
                (frows_in, frows),
                (fcols_in, fcols),
            )
        )
    ]
    index_load, offset_load, frows_load, fcols_load = others
    col_loads = [
        pltpu.make_async_copy(
            col_in.at[:, pl.ds(b * contrib, contrib)], col_taper.at[b], load_sem.at[corr * n_chunk + 4 + b]
        )
        for b in range(sub_cols)
    ]
    row_loads = [
        pltpu.make_async_copy(
            row_in.at[:, pl.ds(a * contrib, contrib)],
            row_taper.at[a],
            load_sem.at[corr * n_chunk + 4 + sub_cols + a],
        )
        for a in range(sub_rows)
    ]
    for load in x_loads[:n_chunk] + col_loads + x_loads[n_chunk:] + others + row_loads:
        load.start()

    barrier = pltpu.get_barrier_semaphore()
    for off in range(1, n_strip):
        pl.semaphore_signal(
            barrier, inc=1, device_id={"strip": lax.rem(s_me + off, n_strip)}, device_id_type=MESH
        )
    near = jnp.minimum(f_me, 1) + jnp.minimum(n_facet - 1 - f_me, 1)

    def signal_near(sem):
        @pl.when(f_me > 0)
        def _():
            pl.semaphore_signal(sem, inc=1, device_id={"facet": f_me - 1}, device_id_type=MESH)

        @pl.when(f_me < n_facet - 1)
        def _():
            pl.semaphore_signal(sem, inc=1, device_id={"facet": f_me + 1}, device_id_type=MESH)

    signal_near(barrier)
    fill_bands(taps_ref, pad_ref, across_ref, down_ref, width, chunks)
    y_ref[:, :, 0:LANES] = jnp.zeros((scales, tall, LANES), y_ref.dtype)
    y_ref[:, :, LANES + side : 2 * LANES + side] = jnp.zeros((scales, tall, LANES), y_ref.dtype)
    col_perm = [lax.rem(owner_ref[b], n_strip) for b in range(sub_cols)]
    row_perm = [lax.div(owner_ref[a * sub_cols], n_strip) for a in range(sub_rows)]

    strip_copies = []
    for n_part in range(corr * n_chunk):
        c, h = divmod(n_part, n_chunk)
        low, high, x_low, x_high = chunks[h]
        x_loads[n_part].wait()
        for s in range(scales):
            for n in range(0, side, COL_TILE):
                y_ref[s, :, LANES + n : LANES + n + COL_TILE] = mm(
                    across_ref[h, s], x_buf[c, s, x_low:x_high, n : n + COL_TILE]
                ).astype(y_ref.dtype)

        def one_tile(tile, carry):
            first = pl.multiple_of(tile * COL_TILE, COL_TILE)
            smoothed = jnp.zeros((tall, COL_TILE), jnp.float32)
            for s in range(scales):
                smoothed += mm(y_ref[s, :, pl.ds(first, COL_TILE + 2 * LANES)], down_ref[s])
            smooth_ref[:, pl.ds(first, COL_TILE)] = smoothed.astype(smooth_ref.dtype)
            return carry

        lax.fori_loop(0, tiles, one_tile, 0, unroll=2)
        if n_part == 0:
            for load in col_loads:
                load.wait()
            pl.semaphore_wait(barrier, n_strip - 1 + near)
            signal_near(wave_sem.at[0])
        for first in range(1, n_strip + 1, 2):
            peers = [lax.rem(s_me + off, n_strip) for off in (first, first + 1)]
            pair = jnp.concatenate([col_taper[position_of(col_perm, peer)] for peer in peers], axis=1)
            got = mm(smooth_ref[...], pair).astype(stage.dtype)
            for n, peer in enumerate(peers):
                off = first + n
                part = got[:, n * contrib : (n + 1) * contrib]
                if off == n_strip:
                    grouped[s_me, n_part] = part
                    continue
                stage[n_part, off] = part
                copy = pltpu.make_async_remote_copy(
                    src_ref=stage.at[n_part, off],
                    dst_ref=grouped.at[s_me, n_part],
                    send_sem=strip_send.at[n_part, off],
                    recv_sem=strip_recv.at[n_part, off],
                    device_id={"strip": peer},
                    device_id_type=MESH,
                )
                copy.start()
                strip_copies.append(copy)
        if n_part == 0:
            continue
        last = n_part == corr * n_chunk - 1
        for wave in range(n_part - 1, n_facet - 2 if last else n_part):
            if wave < n_facet - 2:
                pl.semaphore_wait(wave_sem.at[wave], near)
            if wave + 1 < n_facet - 2:
                signal_near(wave_sem.at[wave + 1])
    for off in range(1, n_strip):
        pl.semaphore_signal(
            ready_sem, inc=1, device_id={"strip": lax.rem(s_me + off, n_strip)}, device_id_type=MESH
        )

    turned[:, r_blocks] = jnp.zeros((corr,) + turned.shape[2:], turned.dtype)
    turned[:, :, q_blocks] = jnp.zeros((corr, r_blocks + 1, ALIGN, LANES), turned.dtype)
    offset_load.wait()
    row_places = lax.broadcasted_iota(jnp.int32, (WIDE, vis), 0)
    col_places = lax.broadcasted_iota(jnp.int32, (TALL, vis), 0)
    factor = -0.5 / (KERNEL_WIDTH * KERNEL_WIDTH)

    def weights(spots, offset):
        delta = spots.astype(jnp.float32) - offset
        inside = (spots >= 0) & (spots < TILE)
        return jnp.where(inside, jnp.exp(factor * (delta * delta)), 0.0)

    def corner(k):
        r, q = corner_ref[0, k], corner_ref[1, k]
        rb = jnp.clip(lax.div(r, LANES), 0, r_blocks - 1)
        qb = jnp.clip(lax.div(q, ALIGN), 0, q_blocks - 2)
        return r - rb * LANES, q - qb * ALIGN, rb, qb

    def one_weight(k, carry):
        r_in, q_in, _, _ = corner(k)
        here = offsets[k]
        row_weights[k] = weights(row_places - r_in, here[0:1]).astype(row_weights.dtype)
        col_weights[k] = weights(col_places - q_in, here[1:2])
        return carry

    lax.fori_loop(0, blocks, one_weight, 0, unroll=2)
    frows_load.wait()
    fcols_load.wait()
    row_mats[...] = jnp.concatenate([frows[f] for f in range(n_facet)], axis=1)
    for load in row_loads:
        load.wait()

    facet_copies = []

    def contribute(c):
        each = n_chunk * (n_strip - 1)
        for copy in strip_copies[c * each : (c + 1) * each]:
            copy.wait()
        head, tail = c * n_chunk, (c + 1) * n_chunk - 1
        flipped = []
        for x in range(n_strip):
            top = grouped[x, head, width : 2 * width]
            bottom = grouped[x, tail, tall - 2 * width : tall - width]
            if x > 0:
                top = plus(top, grouped[x - 1, tail, tall - width : tall])
            if x < n_strip - 1:
                bottom = plus(bottom, grouped[x + 1, head, 0:width])
            middle = []
            for n_part in range(head, tail + 1):
                start = 2 * width if n_part == head else 0
                stop = tall - 2 * width if n_part == tail else tall
                middle.append(grouped[x, n_part, start:stop])
            block = jnp.concatenate([top] + middle + [bottom], axis=0)
            flipped.append(block.T)
        flipped = jnp.concatenate(flipped, axis=1)
        for first in range(1, n_facet + 1, 2):
            peers = [lax.rem(f_me + off, n_facet) for off in (first, first + 1)]
            pair = jnp.concatenate([row_taper[position_of(row_perm, peer)] for peer in peers], axis=1)
            got = mm(flipped, pair).astype(stage2.dtype)
            for n, peer in enumerate(peers):
                off = first + n
                part = got[:, n * contrib : (n + 1) * contrib]
                if off == n_facet:
                    mine[f_me, c] = part
                    continue
                stage2[c, off] = part
                copy = pltpu.make_async_remote_copy(
                    src_ref=stage2.at[c, off],
                    dst_ref=mine.at[f_me, c],
                    send_sem=facet_send.at[c, off],
                    recv_sem=facet_recv.at[c, off],
                    device_id={"facet": peer},
                    device_id_type=MESH,
                )
                copy.start()
                facet_copies.append(copy)

    def degrid(c):
        for copy in facet_copies[c * (n_facet - 1) : (c + 1) * (n_facet - 1)]:
            copy.wait()
        for f in range(n_facet):
            spread[c, :, f * contrib : (f + 1) * contrib] = mm(fcols[f], mine[f, c]).astype(spread.dtype)
        for rb in range(r_blocks):
            turned[c, rb, 0:q_blocks] = (
                lax.dot_general(
                    spread[c],
                    row_mats[rb * LANES : (rb + 1) * LANES],
                    ACROSS,
                    preferred_element_type=jnp.float32,
                )
                .astype(turned.dtype)
                .reshape(q_blocks, ALIGN, LANES)
            )

        def one_block(k, carry):
            _, _, rb, qb = corner(k)
            tile = jnp.concatenate(
                [
                    jnp.concatenate([turned[c, rb + j, qb + i] for j in range(2)], axis=1)
                    for i in range(TALL // ALIGN)
                ],
                axis=0,
            )
            along = mm(tile[:, :WIDE], row_weights[k])
            values[pl.ds(c * blocks + k, 1), :] = jnp.sum(along * col_weights[k], axis=0, keepdims=True)
            return carry

        lax.fori_loop(0, blocks, one_block, 0, unroll=16)

    contribute(0)
    index_load.wait()
    for n in range(corr):
        row = gains_ref[n : n + 1, :]
        product[n] = looked_up(row, index[:, 0, :]) * looked_up(row, index[:, 1, :])
    product_copy = pltpu.make_async_copy(product, product_out, out_sem.at[corr])
    product_copy.start()
    dest = dest_ref[...]
    k_row = lax.broadcasted_iota(jnp.int32, (blocks, blocks), 0)
    k_col = lax.broadcasted_iota(jnp.int32, (blocks, blocks), 1)
    dest_wide = jnp.broadcast_to(dest, (blocks, blocks))
    dest_tall = jnp.sum(jnp.where(k_row == k_col, dest_wide, 0), axis=1, keepdims=True)
    same = (dest_tall == dest_wide) & (k_row < k_col)
    rank = jnp.sum(jnp.where(same, 1, 0), axis=0, keepdims=True)
    target = dest * capacity + rank
    code = jnp.concatenate([target * corr + n for n in range(corr)], axis=1)
    places = lax.broadcasted_iota(jnp.int32, onehot.shape, 0)
    onehot[...] = jnp.where(places == code, 1.0, 0.0).astype(onehot.dtype)
    for c in range(1, corr):
        contribute(c)
        degrid(c - 1)
    degrid(corr - 1)

    outgoing[...] = (
        mm(onehot[...], values[...].astype(jnp.bfloat16))
        .astype(outgoing.dtype)
        .reshape(outgoing.shape)
    )
    pl.semaphore_wait(ready_sem, n_strip - 1)

    vis_copies = []
    for f_off in [n_facet // 2] + [n for n in range(n_facet) if n != n_facet // 2]:
        f_peer = lax.rem(f_me + f_off, n_facet)
        for s_off in range(n_strip):
            if f_off == 0 and s_off == 0:
                continue
            s_peer = lax.rem(s_me + s_off, n_strip)
            off = f_off * n_strip + s_off
            copy = pltpu.make_async_remote_copy(
                src_ref=outgoing.at[f_peer * n_strip + s_peer],
                dst_ref=arrived.at[me],
                send_sem=vis_send.at[off],
                recv_sem=vis_recv.at[off],
                device_id={"facet": f_peer, "strip": s_peer},
                device_id_type=MESH,
            )
            copy.start()
            vis_copies.append(copy)
    own_copy = pltpu.make_async_copy(outgoing.at[me], arrived.at[me], out_sem.at[corr + 1])
    own_copy.start()
    subgrid_copies = [product_copy, own_copy]
    for c in range(corr):
        subgrid[c] = lax.dot_general(
            row_mats[...], spread[c], ACROSS, preferred_element_type=jnp.float32
        ).astype(subgrid.dtype)
        copy = pltpu.make_async_copy(subgrid.at[c], subgrid_out.at[c], out_sem.at[c])
        copy.start()
        subgrid_copies.append(copy)

    for copy in vis_copies:
        copy.wait()
    for copy in subgrid_copies:
        copy.wait()


def close_kernel(
    subgrid_in, arrived_in, product_in, observed_in, subgrid_out, residual_out,
    subgrid, arrived, product, observed, residual, wide, in_sem, out_sem,
):
    parts = subgrid_in.shape[0]
    corr, slots = product.shape[:2]
    small = ((arrived_in, arrived), (product_in, product), (observed_in, observed))
    loads = [
        pltpu.make_async_copy(src, dst, in_sem.at[parts + n]) for n, (src, dst) in enumerate(small)
    ]
    cut_loads = [
        pltpu.make_async_copy(subgrid_in.at[n], subgrid.at[n], in_sem.at[n]) for n in range(parts)
    ]
    stores = [
        pltpu.make_async_copy(subgrid.at[n], subgrid_out.at[n], out_sem.at[n]) for n in range(parts)
    ]
    for load in loads + cut_loads:
        load.start()
    for load in loads:
        load.wait()
    wide[...] = arrived[...].astype(jnp.float32).reshape(wide.shape)
    for c in range(corr):
        placed = wide[pl.ds(c, slots, stride=corr), :]
        residual[:, c, :] = observed[:, c, :] - product[c] * placed
    stores.append(pltpu.make_async_copy(residual, residual_out, out_sem.at[parts]))
    stores[-1].start()
    for load, store in zip(cut_loads, stores):
        load.wait()
        store.start()
    for store in stores:
        store.wait()


def closed(subgrid, arrived, product, observed):
    parts = 4
    cut = subgrid.reshape(parts, -1, subgrid.shape[-1])
    remote = pl.BlockSpec(memory_space=pl.ANY)
    a, b = pl.pallas_call(
        close_kernel,
        in_specs=[remote] * 4,
        out_specs=[remote, remote],
        out_shape=[
            jax.ShapeDtypeStruct(cut.shape, cut.dtype),
            jax.ShapeDtypeStruct(observed.shape, observed.dtype),
        ],
        scratch_shapes=[
            pltpu.VMEM(cut.shape, cut.dtype),
            pltpu.VMEM(arrived.shape, arrived.dtype),
            pltpu.VMEM(product.shape, product.dtype),
            pltpu.VMEM(observed.shape, observed.dtype),
            pltpu.VMEM(observed.shape, observed.dtype),
            pltpu.VMEM((arrived.shape[0] * arrived.shape[1], arrived.shape[2]), jnp.float32),
            pltpu.SemaphoreType.DMA((parts + 3,)),
            pltpu.SemaphoreType.DMA((parts + 1,)),
        ],
        name="closed",
    )(cut, arrived, product, observed)
    return a.reshape(subgrid.shape), b


def on_device(
    sky_components,
    scale_kernels,
    row_taper,
    col_taper,
    finish_rows,
    finish_cols,
    subgrid_owner,
    block_cell,
    vis_offset,
    block_owner,
    observed,
    antenna_pair_index,
    gains,
):
    n_facet = lax.axis_size("facet")
    n_strip = lax.axis_size("strip")
    devices = n_facet * n_strip
    comp = sky_components[0]
    corr, scales, rows, side = comp.shape
    chunks = row_chunks(rows, (scale_kernels.shape[1] - 1) // 2)
    n_chunk = len(chunks)
    tall = chunks[0][1] - chunks[0][0]
    sub_side, contrib = finish_cols.shape[1], finish_cols.shape[2]
    blocks, _, vis = vis_offset.shape
    sub_rows, sub_cols = row_taper.shape[2] // contrib, col_taper.shape[2] // contrib
    slots = observed.shape[0]
    per_device = slots // devices * corr
    whole = pl.BlockSpec(memory_space=pltpu.VMEM)
    scalars = pl.BlockSpec(memory_space=pltpu.SMEM)
    remote = pl.BlockSpec(memory_space=pl.ANY)
    bf16, f32 = jnp.bfloat16, jnp.float32
    dma = pltpu.SemaphoreType.DMA
    subgrid, arrived, product = pl.pallas_call(
        functools.partial(whole_kernel, n_facet, n_strip),
        in_specs=[scalars, scalars, whole, whole, whole] + [remote] * 7,
        out_specs=[remote] * 3,
        out_shape=[
            jax.ShapeDtypeStruct((corr, sub_side, sub_side), bf16),
            jax.ShapeDtypeStruct((devices, per_device, vis), bf16),
            jax.ShapeDtypeStruct((corr, slots, vis), f32),
        ],
        scratch_shapes=[
            pltpu.VMEM((corr, scales, rows, side), bf16),
            pltpu.VMEM((sub_cols, side, contrib), bf16),
            pltpu.VMEM((sub_rows, side, contrib), bf16),
            pltpu.VMEM(finish_rows.shape, bf16),
            pltpu.VMEM(finish_cols.shape, bf16),
            pltpu.VMEM(vis_offset.shape, f32),
            pltpu.VMEM(antenna_pair_index.shape, jnp.int32),
            pltpu.VMEM((scales, BAND), f32),
            pltpu.VMEM((n_chunk, scales, tall, chunks[0][3] - chunks[0][2]), bf16),
            pltpu.VMEM((scales, COL_TILE + 2 * LANES, COL_TILE), bf16),
            pltpu.VMEM((scales, tall, side + 2 * LANES), bf16),
            pltpu.VMEM((tall, side), bf16),
            pltpu.VMEM((corr * n_chunk, n_strip, tall, contrib), bf16),
            pltpu.VMEM((n_strip, corr * n_chunk, tall, contrib), bf16),
            pltpu.VMEM((corr, n_facet, contrib, contrib), bf16),
            pltpu.VMEM((n_facet, corr, contrib, contrib), bf16),
            pltpu.VMEM((sub_side, n_facet * contrib), bf16),
            pltpu.VMEM((corr, sub_side, n_facet * contrib), bf16),
            pltpu.VMEM((corr, sub_side // LANES + 1, sub_side // ALIGN + 1, ALIGN, LANES), bf16),
            pltpu.VMEM((corr, sub_side, sub_side), bf16),
            pltpu.VMEM((blocks, WIDE, vis), bf16),
            pltpu.VMEM((blocks, TALL, vis), f32),
            pltpu.VMEM((devices * per_device, corr * blocks), bf16),
            pltpu.VMEM((corr * blocks, vis), f32),
            pltpu.VMEM((devices, per_device, vis), bf16),
            pltpu.VMEM((corr, slots, vis), f32),
            dma((corr * n_chunk + 4 + sub_cols + sub_rows,)),
            dma((corr * n_chunk, n_strip)),
            dma((corr * n_chunk, n_strip)),
            dma((corr, n_facet)),
            dma((corr, n_facet)),
            dma((devices,)),
            dma((devices,)),
            dma((corr + 2,)),
            pltpu.SemaphoreType.REGULAR,
            pltpu.SemaphoreType.REGULAR((max(n_facet - 2, 1),)),
        ],
        compiler_params=pltpu.CompilerParams(
            collective_id=0, has_side_effects=True, vmem_limit_bytes=60 * 1024 * 1024
        ),
        name="sky_to_residual",
    )(
        subgrid_owner,
        block_cell.T,
        scale_kernels,
        block_owner.reshape(1, blocks),
        gains,
        comp,
        col_taper[0],
        row_taper[0],
        finish_rows,
        finish_cols,
        vis_offset,
        antenna_pair_index,
    )
    subgrid, residual = closed(subgrid, arrived, product, observed)
    return subgrid[None], residual


def solution(mesh):
    placed = (
        P("facet", None, None, "strip", None),
        P(),
        P("facet", None, None),
        P("facet", None, None),
        P(),
        P(),
        P(),
        P(("facet", "strip"), None),
        P(("facet", "strip"), None, None),
        P(("facet", "strip"), None),
        P(("facet", "strip"), None, None),
        P(("facet", "strip"), None, None),
        P(),
    )
    return jax.shard_map(
        on_device,
        mesh=mesh,
        in_specs=placed,
        out_specs=(P(("facet", "strip"), None, None, None), P(("facet", "strip"), None, None)),
        check_vma=False,
    )
```
